32 devices in a mesh: row: 8 (over z, x), col: 4 (over y, core).
Axes of the slice: x: 2, y: 2, z: 4, core: 2. Of those that a mesh axis runs over, the one named last changes fastest.
Arguments:
- solution_field: float32 [32, 32768], P(None, ('row', 'col')), may hold values from -6 to 6
- residual: float32 [32, 32768], P(None, ('row', 'col')), may hold values from -420 to 420
- direction: float32 [32, 32768], P(None, ('row', 'col')), may hold values from -420 to 420
- positions: bfloat16 [2, 32768], P(None, ('row', 'col')), may hold values from -6 to 6
- tile_pairs: int32 [2, 49152], P(None, ('row', 'col')), may hold values from 0 to 63, as said below
- pair_count: int32 [32], P(('row', 'col')), may hold values from 0 to 1536, as said below
Outputs:
- solution_next: float32 [32, 32768], P(None, ('row', 'col'))
- residual_next: float32 [32, 32768], P(None, ('row', 'col'))
- direction_next: float32 [32, 32768], P(None, ('row', 'col'))
The draws below stay inside these ranges and needn't reach their ends.
Inputs may be any that keep to these rules, and one draw needn't show every extreme that they name: `tile_pairs`: row 0 holds local row tiles below 32, row 1 local column tiles below 64. The live pairs of one slot block are distinct and strictly upper (I < J); entries in slots that are not live are in range but carry nothing. `pair_count`: some slot block is full in every draw.
All inputs are finite; a program needn't handle non-finite values.
Results may differ from the reference program's by a relative error of at most 0.007.
Values may be sent and summed in bfloat16 or wider, within the bound.
A program may use at most 64 MiB of HBM per device.

```python
import math
import jax
import jax.numpy as jnp
from jax import lax

TILE = 128
PROBES = 32
TILE_DEV = 8
PAIRS_DEV = 1536
NPTS = 32768
N_ROW = 8
N_COL = 4
DEVICES = 32


def pattern_draw(key):
    key_pick = jax.random.fold_in(key, 11)
    key_rank = jax.random.fold_in(key, 12)
    key_full = jax.random.fold_in(key, 13)
    row_span = N_COL * TILE_DEV
    col_span = N_ROW * TILE_DEV
    device = jnp.arange(DEVICES, dtype=jnp.int32)
    row_dev = device // N_COL
    col_dev = device % N_COL
    row_tile = row_dev[:, None] * row_span + jnp.arange(row_span, dtype=jnp.int32)[None, :]
    col_local = jnp.arange(col_span, dtype=jnp.int32)
    col_tile = (col_local[None, :] // TILE_DEV * N_COL + col_dev[:, None]) * TILE_DEV + col_local[None, :] % TILE_DEV
    cell_total = row_span * col_span
    upper_mask = (row_tile[:, :, None] < col_tile[:, None, :]).reshape(DEVICES, cell_total)
    upper_count = jnp.sum(upper_mask.astype(jnp.int32), axis=1)
    levels = jax.random.randint(key_pick, (DEVICES,), 0, 3)
    full_device = jax.random.randint(key_full, (), 0, N_COL)
    levels = jnp.where(device == full_device, 0, levels)
    divisor = jnp.where(levels == 0, 1, jnp.where(levels == 1, 8, 64))
    counts = jnp.minimum(PAIRS_DEV, upper_count // divisor).astype(jnp.int32)
    spread = max(1, 2 ** 30 // cell_total)
    cell_index = jnp.arange(cell_total, dtype=jnp.int32)[None, :]
    scores = jax.random.randint(key_rank, (DEVICES, cell_total), 0, spread) * cell_total + cell_index
    scores = jnp.where(upper_mask, scores, -1 - cell_index)
    ranked, chosen = lax.top_k(scores, PAIRS_DEV)
    pair_table = jnp.stack([chosen // col_span, chosen % col_span]).reshape(2, DEVICES * PAIRS_DEV)
    return (pair_table.astype(jnp.int32), counts)


def draw_tile_pairs(key, part):
    return pattern_draw(key)[0]


def draw_pair_count(key, part):
    return pattern_draw(key)[1]


def probe_draw(key):
    base_part = jnp.clip(jax.random.normal(jax.random.fold_in(key, 21), (PROBES, NPTS), jnp.float32), -5.0, 5.0)
    noise_part = jnp.clip(jax.random.normal(jax.random.fold_in(key, 22), (PROBES, NPTS), jnp.float32), -5.0, 5.0)
    return (base_part, base_part + 0.6 * noise_part)


def draw_residual(key, part):
    return probe_draw(key)[0]


def draw_direction(key, part):
    return probe_draw(key)[1]


def level_of(key, dims, pieces, low, top_value):
    level = 1.0
    for dim, shards_of in pieces:
        steps = jax.random.uniform(jax.random.fold_in(jax.random.fold_in(key, 6), dim), (shards_of,), jnp.float32, low / len(pieces), top_value / len(pieces))
        level = level * jnp.repeat(jnp.exp(steps), dims[dim] // shards_of).reshape((-1,) + (1,) * (len(dims) - 1 - dim))
    return level


def normal_values(key, dims, scale, most, shards=(), kind=jnp.bfloat16):
    level = level_of(key, dims, shards, -0.22, 0.18) if shards else 1.0
    result = jax.random.normal(key, dims, jnp.float32) * scale * level
    return jnp.minimum(jnp.maximum(result, -most), most).astype(kind)


def setup_inputs(seed: int = 0) -> dict:
    key_list = jax.random.split(jax.random.key(seed), 7)
    return {
        "solution_field": normal_values(key_list[0], (PROBES, NPTS), 1.0, 6.0, ((1, 32),), jnp.float32),
        "residual": draw_residual(jax.random.fold_in(key_list[6], 71), 0),
        "direction": draw_direction(jax.random.fold_in(key_list[6], 71), 0),
        "positions": normal_values(key_list[3], (2, NPTS), 1.0, 6.0, ((1, 32),)),
        "tile_pairs": draw_tile_pairs(jax.random.fold_in(key_list[6], 71), 0),
        "pair_count": draw_pair_count(jax.random.fold_in(key_list[6], 71), 0),
    }


AMPLITUDE = 0.025
NUGGET = 2.0
RADIUS = 1.0
HIGHEST = lax.Precision.HIGHEST

def kernel_tile(near_side, far_side):
    differ = near_side[..., :, None] - far_side[..., None, :]
    distance = jnp.sqrt(lax.optimization_barrier(jnp.sum(differ * differ, axis=0))) / RADIUS
    remain = jnp.maximum(1.0 - distance, 0.0)
    return AMPLITUDE * remain ** 4 * (4.0 * distance + 1.0)

def cross_gram_matrix(former, latter):
    return lax.dot_general(former.astype(jnp.float32), latter.astype(jnp.float32), (((1,), (1,)), ((), ())), precision=HIGHEST, preferred_element_type=jnp.float32)

def apply_left(matrix, vectors):
    return jnp.dot(matrix.T, vectors, precision=HIGHEST)

def symmetric_solve(matrix, target):
    balanced = 0.5 * (matrix + matrix.T)
    factor = jnp.linalg.cholesky(balanced)
    middle = lax.linalg.triangular_solve(factor, target, left_side=True, lower=True)
    return lax.linalg.triangular_solve(factor, middle, left_side=True, lower=True, transpose_a=True)

def reference(solution_field, residual, direction, positions, tile_pairs, pair_count):
    tile_count = NPTS // TILE
    dir_half = lax.optimization_barrier(direction.astype(jnp.bfloat16))
    dir_round = dir_half.astype(jnp.float32).reshape(PROBES, tile_count, TILE)
    coords = positions.astype(jnp.float32).reshape(2, tile_count, TILE)
    total = DEVICES * PAIRS_DEV
    entry = jnp.arange(total, dtype=jnp.int32)
    device = entry // PAIRS_DEV
    slot_index = entry % PAIRS_DEV
    row_dev = device // N_COL
    col_dev = device % N_COL
    row_tile = (row_dev * (N_COL * TILE_DEV) + tile_pairs[0]).astype(jnp.int32)
    col_local = tile_pairs[1]
    col_tile = ((col_local // TILE_DEV * N_COL + col_dev) * TILE_DEV + col_local % TILE_DEV).astype(jnp.int32)
    live_mask = slot_index < pair_count[device]
    block_size = math.gcd(total, 256)
    block_count = total // block_size

    def accumulate(running_totals, packed):
        rows_now, cols_now, live_now = packed
        kernel_block = kernel_tile(coords[:, rows_now], coords[:, cols_now])
        kernel_block = jnp.where(live_now[:, None, None], kernel_block, 0.0).astype(jnp.bfloat16)
        kernel_block = lax.optimization_barrier(kernel_block).astype(jnp.float32)
        forward_step = jnp.einsum('bpq,kbq->kbp', kernel_block, dir_round[:, cols_now], precision=HIGHEST)
        backward = jnp.einsum('bpq,kbp->kbq', kernel_block, dir_round[:, rows_now], precision=HIGHEST)
        running_totals = running_totals.at[:, rows_now].add(forward_step)
        running_totals = running_totals.at[:, cols_now].add(backward)
        return (running_totals, None)
    packed = (row_tile.reshape(block_count, block_size), col_tile.reshape(block_count, block_size), live_mask.reshape(block_count, block_size))
    kernel_sum, unused = lax.scan(accumulate, jnp.zeros((PROBES, tile_count, TILE), jnp.float32), packed)
    diagonal = lax.optimization_barrier(kernel_tile(coords, coords).astype(jnp.bfloat16)).astype(jnp.float32)
    kernel_sum = kernel_sum + jnp.einsum('npq,knq->knp', diagonal, dir_round, precision=HIGHEST)
    applied = NUGGET * direction + kernel_sum.reshape(PROBES, NPTS)
    curvature = cross_gram_matrix(direction, applied)
    crossing = cross_gram_matrix(direction, residual)
    norm_old = cross_gram_matrix(residual, residual)
    step_size = symmetric_solve(curvature, crossing)
    solution_next = solution_field + apply_left(step_size, direction)
    residual_next = residual - apply_left(step_size, applied)
    norm_new = cross_gram_matrix(residual_next, residual_next)
    mix_weight = symmetric_solve(norm_old, norm_new)
    direction_next = residual_next + apply_left(mix_weight, direction)
    return (solution_next, residual_next, direction_next)
```

```python
import functools
import itertools

import jax
import jax.numpy as jnp
from jax import lax
from jax.experimental import pallas as pl
from jax.experimental.pallas import tpu as pltpu
from jax.sharding import PartitionSpec as P

TILE = 128
BLOCK = 2 * TILE

AMPLITUDE = 0.025
NUGGET = 2.0
SCALE = 4.0
FAR_AWAY = 128.0
HIGHEST = lax.Precision.HIGHEST
MESH = pl.DeviceIdType.MESH
F32 = jnp.float32
BF16 = jnp.bfloat16


def cross_gram_matrix(former, latter):
    return lax.dot_general(
        former, latter, (((1,), (1,)), ((), ())), precision=HIGHEST, preferred_element_type=F32
    )


def apply_left(matrix, vectors):
    return jnp.dot(matrix.T, vectors, precision=HIGHEST)


def symmetric_solve(matrix, target):
    balanced = 0.5 * (matrix + matrix.T)
    factor = jnp.linalg.cholesky(balanced)
    middle = lax.linalg.triangular_solve(factor, target, left_side=True, lower=True)
    return lax.linalg.triangular_solve(factor, middle, left_side=True, lower=True, transpose_a=True)


@functools.lru_cache(None)
def cover_of(n_row, n_col):
    every = [(r, c) for r in range(n_row) for c in range(n_col)]

    def minus(a, b):
        return ((a[0] - b[0]) % n_row, (a[1] - b[1]) % n_col)

    def cost(e):
        return min(e[0], n_row - e[0]) + min(e[1], n_col - e[1])

    order = sorted(every[1:], key=lambda e: (cost(e), e))
    total = len(every) - 1
    budget = [20000]

    def extend(chosen, seen, start, size):
        if len(chosen) == size:
            return chosen if len(seen) == total else None
        budget[0] -= 1
        rest = size - len(chosen)
        most = sum(2 * (len(chosen) + k) for k in range(rest))
        if budget[0] < 0 or len(seen) + most < total:
            return None
        for k in range(start, len(order)):
            e = order[k]
            new = {minus(e, x) for x in chosen} | {minus(x, e) for x in chosen}
            found = extend(chosen + [e], seen | new, k + 1, size)
            if found:
                return found
        return None

    size = 1
    while size * (size - 1) < total:
        size += 1
    for k in (size, size + 1):
        budget[0] = 20000
        found = extend([(0, 0)], set(), 0, k)
        if found:
            return tuple(found)
    chosen, seen = [(0, 0)], set()
    while len(seen) < total:
        gains = []
        for e in order:
            new = {minus(e, x) for x in chosen} | {minus(x, e) for x in chosen}
            gains.append((-len((new | seen) - {(0, 0)}), cost(e), e))
        e = min(gains)[2]
        seen |= {minus(e, x) for x in chosen} | {minus(x, e) for x in chosen}
        seen.discard((0, 0))
        chosen.append(e)
    return tuple(chosen)


@functools.lru_cache(None)
def units_of(n_row, n_col):
    cover = cover_of(n_row, n_col)
    found = {}
    for i, j in itertools.permutations(range(len(cover)), 2):
        delta = ((cover[j][0] - cover[i][0]) % n_row, (cover[j][1] - cover[i][1]) % n_col)
        found.setdefault(delta, (i, j))
    return tuple(sorted(found.values(), key=lambda u: (max(u), min(u), u)))


def holders_of(n_row, n_col):
    cover = cover_of(n_row, n_col)
    return sorted({(a[0], b[1]) for a in cover for b in cover} - {(0, 0)})


def group_of(n_row, n_col, tiles):
    group = max(1, TILE // (n_row * tiles))
    while n_col % group:
        group -= 1
    return group


def log2(value):
    assert value & (value - 1) == 0
    return value.bit_length() - 1


def pick(index, values):
    result = jnp.int32(values[0])
    for k, value in enumerate(values[1:], 1):
        result = jnp.where(index == k, jnp.int32(value), result)
    return result


class Ring:
    def __init__(self, n_row, n_col):
        self.n_row, self.n_col = n_row, n_col
        self.row, self.col = lax.axis_index("row"), lax.axis_index("col")

    def plus(self, offset):
        return lax.rem(self.row + offset[0], self.n_row), lax.rem(self.col + offset[1], self.n_col)

    def minus(self, offset):
        return self.plus((self.n_row - offset[0], self.n_col - offset[1]))

    def flat(self, place):
        return place[0] * self.n_col + place[1]

    def greet(self):
        barrier = pltpu.get_barrier_semaphore()
        offsets = [(r, c) for r in range(self.n_row) for c in range(self.n_col)][1:]
        for offset in offsets:
            row, col = self.plus(offset)
            pl.semaphore_signal(
                barrier, inc=1, device_id={"row": row, "col": col}, device_id_type=MESH
            )
        pl.semaphore_wait(barrier, len(offsets))


def remote(source, landing, send_sem, recv_sem, place):
    return pltpu.make_async_remote_copy(
        src_ref=source,
        dst_ref=landing,
        send_sem=send_sem,
        recv_sem=recv_sem,
        device_id={"row": place[0], "col": place[1]},
        device_id_type=MESH,
    )


def one_hot(size, index, live=None):
    slots = index.shape[1]
    hit = lax.broadcasted_iota(jnp.int32, (size, slots), 0) == index
    if live is not None:
        hit = hit & live
    return jnp.where(hit, 1.0, 0.0).astype(BF16)


def pattern(ring, tiles, group, tile_pairs, count):
    rows, cols = tile_pairs[0:1, :], tile_pairs[1:2, :]
    live = lax.broadcasted_iota(jnp.int32, rows.shape, 1) < count
    shift, mask = log2(tiles), tiles - 1
    chunk = rows >> shift
    lanes = group * ring.n_row * tiles
    down = ((chunk >> log2(group)) << shift) + (rows & mask)
    across = (chunk & (group - 1)) * (ring.n_row * tiles) + cols
    table = cross_one_hot(one_hot(ring.n_col // group * tiles, down), one_hot(lanes, across, live))
    near, far = rows - ring.col * tiles, cols - ring.row * tiles
    upper = cross_one_hot(one_hot(tiles, near), one_hot(TILE, far, live))
    lower = cross_one_hot(one_hot(tiles, far, live), one_hot(TILE, near))
    eye = lax.broadcasted_iota(jnp.int32, upper.shape, 0) == lax.broadcasted_iota(
        jnp.int32, upper.shape, 1
    )
    return table, upper + lower + jnp.where(eye, 1.0, 0.0)


def cross_one_hot(former, latter):
    return lax.dot_general(former, latter, (((1,), (1,)), ((), ())), preferred_element_type=F32)


def gather_kernel(
    n_row, n_col, direction, positions, tile_pairs, count, dirs, places, tables, own_table, *sems
):
    ring = Ring(n_row, n_col)
    cover, holders = cover_of(n_row, n_col), holders_of(n_row, n_col)
    tiles = direction.shape[1] // TILE
    group = group_of(n_row, n_col, tiles)
    me = ring.flat((ring.row, ring.col))
    dirs[0] = direction[...].astype(BF16)
    places[0] = positions[...]
    table, own = pattern(ring, tiles, group, tile_pairs, count[0])
    tables[me] = table.reshape(tables.shape[1:]).astype(BF16)
    own_table[...] = own
    ring.greet()
    copies = []
    for k, offset in enumerate(holders):
        place = ring.minus(offset)
        copies.append(remote(tables.at[me], tables.at[me], sems[0].at[k], sems[1].at[k], place))
    for s, offset in enumerate(cover[1:], 1):
        place = ring.minus(offset)
        copies.append(remote(places.at[0], places.at[s], sems[2].at[s], sems[3].at[s], place))
        copies.append(remote(dirs.at[0], dirs.at[s], sems[4].at[s], sems[5].at[s], place))
    for copy in copies:
        copy.start()
    for k, offset in enumerate(holders):
        origin = ring.plus(offset)
        at = tables.at[ring.flat(origin)]
        remote(at, at, sems[0].at[k], sems[1].at[k], origin).wait_recv()
    for s, offset in enumerate(cover[1:], 1):
        origin = ring.plus(offset)
        remote(places.at[0], places.at[s], sems[2].at[s], sems[3].at[s], origin).wait_recv()
        remote(dirs.at[0], dirs.at[s], sems[4].at[s], sems[5].at[s], origin).wait_recv()
    for copy in copies:
        copy.wait_send()


def kernel_of(differ_x, differ_y):
    square = (differ_x * differ_x + differ_y * differ_y).astype(F32)
    square = jnp.minimum(jnp.maximum(square, 1e-20), SCALE * SCALE)
    quad = square * lax.rsqrt(square)
    remain = SCALE - quad
    remain = remain * remain
    return (remain * remain * (quad + 1.0)).astype(BF16)


def times_transposed(vectors, block):
    return lax.dot_general(
        vectors, block, (((1,), (1,)), ((), ())), preferred_element_type=F32
    )


def spread_places(slot, places, near_x, near_y):
    pair = places[slot].astype(F32) * SCALE
    points = pair.shape[1]
    side = lax.broadcasted_iota(jnp.int32, (2, 2 * TILE), 1) // TILE
    pick_side = jnp.where(side == lax.broadcasted_iota(jnp.int32, side.shape, 0), 1.0, 0.0)
    both = lax.dot_general(
        pair.astype(BF16),
        pick_side.astype(BF16),
        (((0,), (0,)), ((), ())),
        preferred_element_type=F32,
    ).astype(BF16)
    near_x[slot] = both[:, :TILE]
    near_y[slot] = both[:, TILE:]


def set_far(slot, mask, places, widen, far_x, far_y):
    pair = places[slot].astype(F32) * SCALE
    on = jnp.dot(mask.astype(BF16), widen[...], preferred_element_type=F32)
    x = (pair[0:1] + FAR_AWAY * (1.0 - on)).astype(BF16)
    for a in range(mask.shape[0]):
        far_x[a] = x[a : a + 1]
    far_y[...] = pair[1:2].astype(BF16)


def block_of(slot, base, tile_row, j, near_x, near_y, far_x, far_y):
    rows = []
    for a in range(2):
        at = pl.ds(pl.multiple_of(base + a * TILE, TILE), TILE)
        x, y = near_x[slot, at, :], near_y[slot, at, :]
        row = []
        for b in range(2):
            across = pl.ds(j * BLOCK + b * TILE, TILE)
            row.append(kernel_of(x - far_x[tile_row + a, :, across], y - far_y[:, across]))
        rows.append(jnp.concatenate(row, axis=1))
    return jnp.concatenate(rows, axis=0)


def pair_kernel(
    n_row, n_col, dirs, places, tables, own_table, parts, own, acc, near_x, near_y, far_x, far_y, widen
):
    ring = Ring(n_row, n_col)
    cover, units = cover_of(n_row, n_col), units_of(n_row, n_col)
    slots, probes, points = dirs.shape
    tiles, blocks = points // TILE, points // BLOCK
    group = group_of(n_row, n_col, tiles)
    scale = AMPLITUDE / 256.0
    acc[...] = jnp.zeros_like(acc)
    lane = lax.broadcasted_iota(jnp.int32, widen.shape, 1) >> log2(TILE)
    widen[...] = jnp.where(lane == lax.broadcasted_iota(jnp.int32, widen.shape, 0), 1.0, 0.0).astype(
        BF16
    )

    @pl.loop(0, slots)
    def _(slot):
        spread_places(slot, places, near_x, near_y)

    set_far(0, own_table[...], places, widen, far_x, far_y)

    @pl.loop(0, blocks)
    def _(i):
        base = pl.multiple_of(i * BLOCK, BLOCK)
        total = jnp.zeros((probes, BLOCK), F32)
        for j in range(blocks):
            block = block_of(0, base, 2 * i, j, near_x, near_y, far_x, far_y)
            total += times_transposed(dirs[0, :, j * BLOCK : (j + 1) * BLOCK], block)
        acc[0, :, pl.ds(base, BLOCK)] += total

    rows_of, cols_of = [o[0] for o in cover], [o[1] for o in cover]

    @pl.loop(0, len(units))
    def _(t):
        i, j = pick(t, [u[0] for u in units]), pick(t, [u[1] for u in units])
        row_i, col_i = ring.plus((pick(i, rows_of), pick(i, cols_of)))
        row_j, col_j = ring.plus((pick(j, rows_of), pick(j, cols_of)))
        swap = (row_i * n_col + col_i - row_j * n_col - col_j + n_row * n_col) // (n_row * n_col)
        low, high = i + swap * (j - i), j + swap * (i - j)
        row_low = row_i + swap * (row_j - row_i)
        row_high = row_j + swap * (row_i - row_j)
        col_low = col_i + swap * (col_j - col_i)
        col_high = col_j + swap * (col_i - col_j)
        table = tables[row_low * n_col + col_high, col_low // group].astype(F32)
        lanes = table.shape[1]
        start = (col_low % group) * (n_row * tiles) + row_high * tiles
        mask = pltpu.roll(table, lax.rem(lanes - start, lanes), 1)
        set_far(high, mask[:, :TILE], places, widen, far_x, far_y)
        half = blocks // 2
        first = swap * half
        forward = [None] * half
        backward = [None] * blocks
        for a in range(half):
            base = pl.multiple_of((first + a) * BLOCK, BLOCK)
            near_vec = dirs[low, :, pl.ds(base, BLOCK)]
            for b in range(blocks):
                block = block_of(low, base, 2 * (first + a), b, near_x, near_y, far_x, far_y)
                ahead = times_transposed(dirs[high, :, b * BLOCK : (b + 1) * BLOCK], block)
                back = jnp.dot(near_vec, block, preferred_element_type=F32)
                forward[a] = ahead if b == 0 else forward[a] + ahead
                backward[b] = back if a == 0 else backward[b] + back
        for a in range(half):
            base = pl.multiple_of((first + a) * BLOCK, BLOCK)
            acc[low, :, pl.ds(base, BLOCK)] += forward[a]
        for b in range(blocks):
            acc[high, :, b * BLOCK : (b + 1) * BLOCK] += backward[b]

    own[...] = scale * acc[0]
    for s in range(1, slots):
        parts[s - 1] = (scale * acc[s]).astype(BF16)


class Exchange:
    def __init__(self, axis, size, source, landing, send_sem, recv_sem):
        self.axis, self.size, self.source, self.landing = axis, size, source, landing
        self.send_sem, self.recv_sem = send_sem, recv_sem
        self.me = lax.axis_index(axis)

    def copy(self, k, source, slot, peer):
        return pltpu.make_async_remote_copy(
            src_ref=source,
            dst_ref=self.landing.at[slot],
            send_sem=self.send_sem.at[k],
            recv_sem=self.recv_sem.at[k],
            device_id={self.axis: peer},
            device_id_type=MESH,
        )

    def outgoing(self, k):
        peer = lax.rem(self.me + k, self.size)
        return self.copy(k, self.source, self.me, peer)

    def start(self):
        for k in range(1, self.size):
            self.outgoing(k).start()

    def wait_recv(self):
        for k in range(1, self.size):
            origin = lax.rem(self.me + self.size - k, self.size)
            self.copy(k, self.landing.at[origin], origin, origin).wait_recv()

    def wait_send(self):
        for k in range(1, self.size):
            self.outgoing(k).wait_send()


def image_kernel(
    n_row,
    n_col,
    parts,
    own,
    direction,
    residual,
    applied,
    gram,
    land,
    gram_own,
    gram_half,
    gram_col,
    gram_row,
    *sems,
):
    ring = Ring(n_row, n_col)
    cover = cover_of(n_row, n_col)
    ring.greet()
    sends = []
    for s, offset in enumerate(cover[1:], 1):
        place = ring.plus(offset)
        sends.append(
            remote(parts.at[s - 1], land.at[s - 1], sems[0].at[s - 1], sems[1].at[s - 1], place)
        )
    for copy in sends:
        copy.start()
    total = own[...] + NUGGET * direction[...]
    for s, offset in enumerate(cover[1:], 1):
        place = ring.minus(offset)
        remote(
            parts.at[s - 1], land.at[s - 1], sems[0].at[s - 1], sems[1].at[s - 1], place
        ).wait_recv()
        total += land[s - 1].astype(F32)
    image = total
    applied[...] = image
    left = jnp.concatenate([image, residual[...]], axis=0)
    right = jnp.concatenate([left, direction[...]], axis=0)
    product = cross_gram_matrix(left, right)
    lanes = gram_own.shape[1] - product.shape[1]
    gram_own[...] = jnp.concatenate([product, jnp.zeros((product.shape[0], lanes), F32)], axis=1)
    gram_over_col = Exchange("col", n_col, gram_own, gram_col, sems[2], sems[3])
    gram_over_col.start()
    gram_over_col.wait_recv()
    half = gram_own[...]
    for k in range(1, n_col):
        half += gram_col[lax.rem(ring.col + k, n_col)]
    gram_half[...] = half
    gram_over_row = Exchange("row", n_row, gram_half, gram_row, sems[4], sems[5])
    gram_over_row.start()
    gram_over_row.wait_recv()
    whole = gram_half[...]
    for k in range(1, n_row):
        whole += gram_row[lax.rem(ring.row + k, n_row)]
    gram[...] = whole
    for copy in sends:
        copy.wait_send()
    gram_over_col.wait_send()
    gram_over_row.wait_send()


def on_device(solution_field, residual, direction, positions, tile_pairs, pair_count):
    probes, points = direction.shape
    n_row, n_col = lax.axis_size("row"), lax.axis_size("col")
    cover, holders = cover_of(n_row, n_col), holders_of(n_row, n_col)
    slots, tiles = len(cover), points // TILE
    group = group_of(n_row, n_col, tiles)
    lanes = group * n_row * tiles
    vmem = pl.BlockSpec(memory_space=pltpu.VMEM)
    smem = pl.BlockSpec(memory_space=pltpu.SMEM)
    dma = pltpu.SemaphoreType.DMA
    dirs, places, tables, own_table = pl.pallas_call(
        functools.partial(gather_kernel, n_row, n_col),
        out_shape=(
            jax.ShapeDtypeStruct((slots, probes, points), BF16),
            jax.ShapeDtypeStruct((slots, 2, points), BF16),
            jax.ShapeDtypeStruct((n_row * n_col, n_col // group, tiles, lanes), BF16),
            jax.ShapeDtypeStruct((tiles, TILE), F32),
        ),
        in_specs=[vmem, vmem, vmem, smem],
        out_specs=(vmem,) * 4,
        scratch_shapes=[dma((len(holders),))] * 2 + [dma((slots,))] * 4,
        compiler_params=pltpu.CompilerParams(collective_id=0, has_side_effects=True),
        name="gather",
    )(direction, positions, tile_pairs, pair_count)
    parts, own = pl.pallas_call(
        functools.partial(pair_kernel, n_row, n_col),
        out_shape=(
            jax.ShapeDtypeStruct((slots - 1, probes, points), BF16),
            jax.ShapeDtypeStruct((probes, points), F32),
        ),
        in_specs=[vmem] * 4,
        out_specs=(vmem,) * 2,
        scratch_shapes=[
            pltpu.VMEM((slots, probes, points), F32),
            pltpu.VMEM((slots, points, TILE), BF16),
            pltpu.VMEM((slots, points, TILE), BF16),
            pltpu.VMEM((tiles, 1, points), BF16),
            pltpu.VMEM((1, points), BF16),
            pltpu.VMEM((TILE, points), BF16),
        ],
        name="pairs",
    )(dirs, places, tables, own_table)
    applied, gram = pl.pallas_call(
        functools.partial(image_kernel, n_row, n_col),
        out_shape=(
            jax.ShapeDtypeStruct((probes, points), F32),
            jax.ShapeDtypeStruct((2 * probes, TILE), F32),
        ),
        in_specs=[vmem] * 4,
        out_specs=(vmem, vmem),
        scratch_shapes=[
            pltpu.VMEM((slots - 1, probes, points), BF16),
            pltpu.VMEM((2 * probes, TILE), F32),
            pltpu.VMEM((2 * probes, TILE), F32),
            pltpu.VMEM((n_col, 2 * probes, TILE), F32),
            pltpu.VMEM((n_row, 2 * probes, TILE), F32),
            dma((slots - 1,)),
            dma((slots - 1,)),
            dma((n_col,)),
            dma((n_col,)),
            dma((n_row,)),
            dma((n_row,)),
        ],
        compiler_params=pltpu.CompilerParams(collective_id=1, has_side_effects=True),
        name="image",
    )(parts, own, direction, residual)
    square, image_resid = gram[:probes, :probes], gram[:probes, probes : 2 * probes]
    norm_old = gram[probes:, probes : 2 * probes]
    curvature = gram[:probes, 2 * probes : 3 * probes].T
    crossing = gram[probes:, 2 * probes : 3 * probes].T
    step_size = symmetric_solve(curvature, crossing)
    residual_next = residual - apply_left(step_size, applied)
    shifted = jnp.dot(step_size.T, image_resid, precision=HIGHEST)
    quadratic = jnp.dot(
        step_size.T, jnp.dot(square, step_size, precision=HIGHEST), precision=HIGHEST
    )
    norm_new = norm_old - shifted - shifted.T + quadratic
    solution_next = solution_field + apply_left(step_size, direction)
    mix_weight = symmetric_solve(norm_old, norm_new)
    direction_next = residual_next + apply_left(mix_weight, direction)
    return (solution_next, residual_next, direction_next)


def solution(mesh):
    whole = P(None, ("row", "col"))
    return jax.shard_map(
        on_device,
        mesh=mesh,
        in_specs=(whole, whole, whole, whole, whole, P(("row", "col"))),
        out_specs=(whole, whole, whole),
        check_vma=False,
    )
```

```python
import functools
import itertools

import jax
import jax.numpy as jnp
from jax import lax
from jax.experimental import pallas as pl
from jax.experimental.pallas import tpu as pltpu
from jax.sharding import PartitionSpec as P

TILE = 128
BLOCK = 2 * TILE

AMPLITUDE = 0.025
NUGGET = 2.0
SCALE = 4.0
FAR_AWAY = 128.0
HIGHEST = lax.Precision.HIGHEST
MESH = pl.DeviceIdType.MESH
F32 = jnp.float32
BF16 = jnp.bfloat16


def cross_gram_matrix(former, latter):
    return lax.dot_general(
        former, latter, (((1,), (1,)), ((), ())), precision=HIGHEST, preferred_element_type=F32
    )


def apply_left(matrix, vectors):
    return jnp.dot(matrix.T, vectors, precision=HIGHEST)


def symmetric_solve(matrix, target):
    balanced = 0.5 * (matrix + matrix.T)
    factor = jnp.linalg.cholesky(balanced)
    middle = lax.linalg.triangular_solve(factor, target, left_side=True, lower=True)
    return lax.linalg.triangular_solve(factor, middle, left_side=True, lower=True, transpose_a=True)


@functools.lru_cache(None)
def cover_of(n_row, n_col):
    every = [(r, c) for r in range(n_row) for c in range(n_col)]

    def minus(a, b):
        return ((a[0] - b[0]) % n_row, (a[1] - b[1]) % n_col)

    def cost(e):
        return min(e[0], n_row - e[0]) + min(e[1], n_col - e[1])

    order = sorted(every[1:], key=lambda e: (cost(e), e))
    total = len(every) - 1
    budget = [20000]

    def extend(chosen, seen, start, size):
        if len(chosen) == size:
            return chosen if len(seen) == total else None
        budget[0] -= 1
        rest = size - len(chosen)
        most = sum(2 * (len(chosen) + k) for k in range(rest))
        if budget[0] < 0 or len(seen) + most < total:
            return None
        for k in range(start, len(order)):
            e = order[k]
            new = {minus(e, x) for x in chosen} | {minus(x, e) for x in chosen}
            found = extend(chosen + [e], seen | new, k + 1, size)
            if found:
                return found
        return None

    size = 1
    while size * (size - 1) < total:
        size += 1
    for k in (size, size + 1):
        budget[0] = 20000
        found = extend([(0, 0)], set(), 0, k)
        if found:
            return tuple(found)
    chosen, seen = [(0, 0)], set()
    while len(seen) < total:
        gains = []
        for e in order:
            new = {minus(e, x) for x in chosen} | {minus(x, e) for x in chosen}
            gains.append((-len((new | seen) - {(0, 0)}), cost(e), e))
        e = min(gains)[2]
        seen |= {minus(e, x) for x in chosen} | {minus(x, e) for x in chosen}
        seen.discard((0, 0))
        chosen.append(e)
    return tuple(chosen)


@functools.lru_cache(None)
def units_of(n_row, n_col):
    cover = cover_of(n_row, n_col)
    found = {}
    for i, j in itertools.permutations(range(len(cover)), 2):
        delta = ((cover[j][0] - cover[i][0]) % n_row, (cover[j][1] - cover[i][1]) % n_col)
        found.setdefault(delta, (i, j))
    return tuple(sorted(found.values(), key=lambda u: (max(u), min(u), u)))


def holders_of(n_row, n_col):
    cover = cover_of(n_row, n_col)
    return sorted({(a[0], b[1]) for a in cover for b in cover} - {(0, 0)})


def group_of(n_row, n_col, tiles):
    group = max(1, TILE // (n_row * tiles))
    while n_col % group:
        group -= 1
    return group


def log2(value):
    assert value & (value - 1) == 0
    return value.bit_length() - 1


def pick(index, values):
    result = jnp.int32(values[0])
    for k, value in enumerate(values[1:], 1):
        result = jnp.where(index == k, jnp.int32(value), result)
    return result


class Ring:
    def __init__(self, n_row, n_col):
        self.n_row, self.n_col = n_row, n_col
        self.row, self.col = lax.axis_index("row"), lax.axis_index("col")

    def plus(self, offset):
        return lax.rem(self.row + offset[0], self.n_row), lax.rem(self.col + offset[1], self.n_col)

    def minus(self, offset):
        return self.plus((self.n_row - offset[0], self.n_col - offset[1]))

    def flat(self, place):
        return place[0] * self.n_col + place[1]

    def greet(self):
        barrier = pltpu.get_barrier_semaphore()
        offsets = [(r, c) for r in range(self.n_row) for c in range(self.n_col)][1:]
        for offset in offsets:
            row, col = self.plus(offset)
            pl.semaphore_signal(
                barrier, inc=1, device_id={"row": row, "col": col}, device_id_type=MESH
            )
        pl.semaphore_wait(barrier, len(offsets))


def remote(source, landing, send_sem, recv_sem, place):
    return pltpu.make_async_remote_copy(
        src_ref=source,
        dst_ref=landing,
        send_sem=send_sem,
        recv_sem=recv_sem,
        device_id={"row": place[0], "col": place[1]},
        device_id_type=MESH,
    )


def one_hot(size, index, live=None):
    slots = index.shape[1]
    hit = lax.broadcasted_iota(jnp.int32, (size, slots), 0) == index
    if live is not None:
        hit = hit & live
    return jnp.where(hit, 1.0, 0.0).astype(BF16)


def pattern(ring, tiles, group, tile_pairs, count):
    rows, cols = tile_pairs[0:1, :], tile_pairs[1:2, :]
    live = lax.broadcasted_iota(jnp.int32, rows.shape, 1) < count
    shift, mask = log2(tiles), tiles - 1
    chunk = rows >> shift
    lanes = group * ring.n_row * tiles
    down = ((chunk >> log2(group)) << shift) + (rows & mask)
    across = (chunk & (group - 1)) * (ring.n_row * tiles) + cols
    table = cross_one_hot(one_hot(ring.n_col // group * tiles, down), one_hot(lanes, across, live))
    near, far = rows - ring.col * tiles, cols - ring.row * tiles
    upper = cross_one_hot(one_hot(tiles, near), one_hot(TILE, far, live))
    lower = cross_one_hot(one_hot(tiles, far, live), one_hot(TILE, near))
    eye = lax.broadcasted_iota(jnp.int32, upper.shape, 0) == lax.broadcasted_iota(
        jnp.int32, upper.shape, 1
    )
    return table, upper + lower + jnp.where(eye, 1.0, 0.0)


def cross_one_hot(former, latter):
    return lax.dot_general(former, latter, (((1,), (1,)), ((), ())), preferred_element_type=F32)


def kernel_of(differ_x, differ_y):
    square = (differ_x * differ_x + differ_y * differ_y).astype(F32)
    square = jnp.minimum(jnp.maximum(square, 1e-20), SCALE * SCALE)
    quad = square * lax.rsqrt(square)
    remain = SCALE - quad
    remain = remain * remain
    return (remain * remain * (quad + 1.0)).astype(BF16)


def times_transposed(vectors, block):
    return lax.dot_general(
        vectors, block, (((1,), (1,)), ((), ())), preferred_element_type=F32
    )


def spread_places(slot, places, near_x, near_y):
    pair = places[slot].astype(F32) * SCALE
    points = pair.shape[1]
    side = lax.broadcasted_iota(jnp.int32, (2, 2 * TILE), 1) // TILE
    pick_side = jnp.where(side == lax.broadcasted_iota(jnp.int32, side.shape, 0), 1.0, 0.0)
    both = lax.dot_general(
        pair.astype(BF16),
        pick_side.astype(BF16),
        (((0,), (0,)), ((), ())),
        preferred_element_type=F32,
    ).astype(BF16)
    near_x[slot] = both[:, :TILE]
    near_y[slot] = both[:, TILE:]


def set_far(slot, mask, places, widen, far_x, far_y):
    pair = places[slot].astype(F32) * SCALE
    on = jnp.dot(mask.astype(BF16), widen[...], preferred_element_type=F32)
    x = (pair[0:1] + FAR_AWAY * (1.0 - on)).astype(BF16)
    for a in range(mask.shape[0]):
        far_x[a] = x[a : a + 1]
    far_y[...] = pair[1:2].astype(BF16)


def block_of(slot, base, tile_row, j, near_x, near_y, far_x, far_y):
    rows = []
    for a in range(2):
        at = pl.ds(pl.multiple_of(base + a * TILE, TILE), TILE)
        x, y = near_x[slot, at, :], near_y[slot, at, :]
        row = []
        for b in range(2):
            across = pl.ds(j * BLOCK + b * TILE, TILE)
            row.append(kernel_of(x - far_x[tile_row + a, :, across], y - far_y[:, across]))
        rows.append(jnp.concatenate(row, axis=1))
    return jnp.concatenate(rows, axis=0)


def batches_of(n_row, n_col):
    cover, units = cover_of(n_row, n_col), list(units_of(n_row, n_col))
    result, waited = [], {0}
    for slot in range(1, len(cover)):
        mine = sorted((u for u in units if slot in u), key=lambda u: (sum(u) - slot, u))
        units = [u for u in units if slot not in u]
        cut = [u for u in mine if sum(u) - slot <= len(cover) // 2]
        pieces = [cut, mine[len(cut) :]] if slot == 1 else [mine]
        pieces = [piece for piece in pieces if piece]
        for k, piece in enumerate(pieces):
            need = sorted({s for u in piece for s in u} - waited)
            waited |= set(need)
            result.append((need, piece, slot if k == len(pieces) - 1 else None))
    return result


def step_kernel(
    n_row,
    n_col,
    direction,
    residual,
    positions,
    tile_pairs,
    count,
    applied,
    gram,
    dirs,
    places,
    tables,
    acc,
    near_x,
    near_y,
    far_x,
    far_y,
    widen,
    parts,
    land,
    gram_own,
    gram_half,
    gram_col,
    gram_row,
    *sems,
):
    ring = Ring(n_row, n_col)
    cover, holders = cover_of(n_row, n_col), holders_of(n_row, n_col)
    slots, probes, points = dirs.shape
    tiles, blocks = points // TILE, points // BLOCK
    half = blocks // 2
    group = group_of(n_row, n_col, tiles)
    scale = AMPLITUDE / 256.0
    me = ring.flat((ring.row, ring.col))

    dirs[0] = direction[...].astype(BF16)
    places[0] = positions[...]
    table, own_table = pattern(ring, tiles, group, tile_pairs, count[0])
    tables[me] = table.reshape(tables.shape[1:]).astype(BF16)
    ring.greet()
    sends = []
    for s, offset in enumerate(cover[1:], 1):
        place = ring.minus(offset)
        sends.append(remote(places.at[0], places.at[s], sems[2].at[s], sems[3].at[s], place))
    for k, offset in enumerate(holders):
        place = ring.minus(offset)
        sends.append(remote(tables.at[me], tables.at[me], sems[0].at[k], sems[1].at[k], place))
    for s, offset in enumerate(cover[1:], 1):
        place = ring.minus(offset)
        sends.append(remote(dirs.at[0], dirs.at[s], sems[4].at[s], sems[5].at[s], place))
    for copy in sends:
        copy.start()

    def exchanges(part):
        base = 8 + 4 * part
        over_col = Exchange(
            "col", n_col, gram_own.at[part], gram_col.at[part], sems[base], sems[base + 1]
        )
        over_row = Exchange(
            "row", n_row, gram_half.at[part], gram_row.at[part], sems[base + 2], sems[base + 3]
        )
        return over_col, over_row

    def sum_cols(part):
        total = gram_own[part]
        for k in range(1, n_col):
            total += gram_col[part, lax.rem(ring.col + k, n_col)]
        gram_half[part] = total

    def sum_rows(part):
        total = gram_half[part]
        for k in range(1, n_row):
            total += gram_row[part, lax.rem(ring.row + k, n_row)]
        gram[part * probes : (part + 1) * probes] = total

    def padded(product, before):
        widths = (before, TILE - before - product.shape[1])
        sides = [[jnp.zeros((probes, n), F32)] if n else [] for n in widths]
        return jnp.concatenate(sides[0] + [product] + sides[1], axis=1)

    early_col, early_row = exchanges(1)
    late_col, late_row = exchanges(0)
    sides = jnp.concatenate([residual[...], direction[...]], axis=0)
    gram_own[1] = padded(cross_gram_matrix(residual[...], sides), probes)
    early_col.start()

    acc[...] = jnp.zeros_like(acc)
    lane = lax.broadcasted_iota(jnp.int32, widen.shape, 1) >> log2(TILE)
    widen[...] = jnp.where(lane == lax.broadcasted_iota(jnp.int32, widen.shape, 0), 1.0, 0.0).astype(
        BF16
    )
    spread_places(0, places, near_x, near_y)
    set_far(0, own_table, places, widen, far_x, far_y)

    @pl.loop(0, blocks)
    def _(i):
        base = pl.multiple_of(i * BLOCK, BLOCK)
        total = jnp.zeros((probes, BLOCK), F32)
        for j in range(blocks):
            block = block_of(0, base, 2 * i, j, near_x, near_y, far_x, far_y)
            total += times_transposed(dirs[0, :, j * BLOCK : (j + 1) * BLOCK], block)
        acc[0, :, pl.ds(base, BLOCK)] += total

    for s, offset in enumerate(cover[1:], 1):
        origin = ring.plus(offset)
        remote(places.at[0], places.at[s], sems[2].at[s], sems[3].at[s], origin).wait_recv()

    @pl.loop(1, slots)
    def _(slot):
        spread_places(slot, places, near_x, near_y)

    for k, offset in enumerate(holders):
        origin = ring.plus(offset)
        at = tables.at[ring.flat(origin)]
        remote(at, at, sems[0].at[k], sems[1].at[k], origin).wait_recv()

    rows_of, cols_of = [o[0] for o in cover], [o[1] for o in cover]

    def unit(i, j):
        row_i, col_i = ring.plus((pick(i, rows_of), pick(i, cols_of)))
        row_j, col_j = ring.plus((pick(j, rows_of), pick(j, cols_of)))
        swap = (row_i * n_col + col_i - row_j * n_col - col_j + n_row * n_col) // (n_row * n_col)
        low, high = i + swap * (j - i), j + swap * (i - j)
        row_low = row_i + swap * (row_j - row_i)
        row_high = row_j + swap * (row_i - row_j)
        col_low = col_i + swap * (col_j - col_i)
        col_high = col_j + swap * (col_i - col_j)
        table = tables[row_low * n_col + col_high, col_low // group].astype(F32)
        lanes = table.shape[1]
        start = (col_low % group) * (n_row * tiles) + row_high * tiles
        mask = pltpu.roll(table, lax.rem(lanes - start, lanes), 1)
        set_far(high, mask[:, :TILE], places, widen, far_x, far_y)
        first = swap * half
        forward = [None] * half
        backward = [None] * blocks
        for a in range(half):
            base = pl.multiple_of((first + a) * BLOCK, BLOCK)
            near_vec = dirs[low, :, pl.ds(base, BLOCK)]
            for b in range(blocks):
                block = block_of(low, base, 2 * (first + a), b, near_x, near_y, far_x, far_y)
                ahead = times_transposed(dirs[high, :, b * BLOCK : (b + 1) * BLOCK], block)
                back = jnp.dot(near_vec, block, preferred_element_type=F32)
                forward[a] = ahead if b == 0 else forward[a] + ahead
                backward[b] = back if a == 0 else backward[b] + back
        for a in range(half):
            base = pl.multiple_of((first + a) * BLOCK, BLOCK)
            acc[low, :, pl.ds(base, BLOCK)] += forward[a]
        for b in range(blocks):
            acc[high, :, b * BLOCK : (b + 1) * BLOCK] += backward[b]

    for k, (need, units, complete) in enumerate(batches_of(n_row, n_col)):
        for s in need:
            origin = ring.plus(cover[s])
            remote(dirs.at[0], dirs.at[s], sems[4].at[s], sems[5].at[s], origin).wait_recv()

        @pl.loop(0, len(units))
        def _(t):
            unit(pick(t, [u[0] for u in units]), pick(t, [u[1] for u in units]))

        if k == 0:
            early_col.wait_recv()
            sum_cols(1)
            early_row.start()
        if k == 1:
            early_row.wait_recv()
            sum_rows(1)
        if complete is not None:
            s = complete - 1
            parts[s] = (scale * acc[complete]).astype(BF16)
            copy = remote(
                parts.at[s], land.at[s], sems[6].at[s], sems[7].at[s], ring.plus(cover[complete])
            )
            copy.start()
            sends.append(copy)

    image = scale * acc[0] + NUGGET * direction[...]
    for s, offset in enumerate(cover[1:]):
        origin = ring.minus(offset)
        remote(parts.at[s], land.at[s], sems[6].at[s], sems[7].at[s], origin).wait_recv()
        image += land[s].astype(F32)
    applied[...] = image
    gram_own[0] = padded(cross_gram_matrix(image, jnp.concatenate([image, sides], axis=0)), 0)
    late_col.start()
    late_col.wait_recv()
    sum_cols(0)
    late_row.start()
    late_row.wait_recv()
    sum_rows(0)
    for copy in sends + [early_col, early_row, late_col, late_row]:
        copy.wait_send()


class Exchange:
    def __init__(self, axis, size, source, landing, send_sem, recv_sem):
        self.axis, self.size, self.source, self.landing = axis, size, source, landing
        self.send_sem, self.recv_sem = send_sem, recv_sem
        self.me = lax.axis_index(axis)

    def copy(self, k, source, slot, peer):
        return pltpu.make_async_remote_copy(
            src_ref=source,
            dst_ref=self.landing.at[slot],
            send_sem=self.send_sem.at[k],
            recv_sem=self.recv_sem.at[k],
            device_id={self.axis: peer},
            device_id_type=MESH,
        )

    def outgoing(self, k):
        peer = lax.rem(self.me + k, self.size)
        return self.copy(k, self.source, self.me, peer)

    def start(self):
        for k in range(1, self.size):
            self.outgoing(k).start()

    def wait_recv(self):
        for k in range(1, self.size):
            origin = lax.rem(self.me + self.size - k, self.size)
            self.copy(k, self.landing.at[origin], origin, origin).wait_recv()

    def wait_send(self):
        for k in range(1, self.size):
            self.outgoing(k).wait_send()


def on_device(solution_field, residual, direction, positions, tile_pairs, pair_count):
    probes, points = direction.shape
    n_row, n_col = lax.axis_size("row"), lax.axis_size("col")
    cover, holders = cover_of(n_row, n_col), holders_of(n_row, n_col)
    slots, tiles = len(cover), points // TILE
    group = group_of(n_row, n_col, tiles)
    lanes = group * n_row * tiles
    vmem = pl.BlockSpec(memory_space=pltpu.VMEM)
    smem = pl.BlockSpec(memory_space=pltpu.SMEM)
    dma = pltpu.SemaphoreType.DMA
    applied, gram = pl.pallas_call(
        functools.partial(step_kernel, n_row, n_col),
        out_shape=(
            jax.ShapeDtypeStruct((probes, points), F32),
            jax.ShapeDtypeStruct((2 * probes, TILE), F32),
        ),
        in_specs=[vmem] * 4 + [smem],
        out_specs=(vmem, vmem),
        scratch_shapes=[
            pltpu.VMEM((slots, probes, points), BF16),
            pltpu.VMEM((slots, 2, points), BF16),
            pltpu.VMEM((n_row * n_col, n_col // group, tiles, lanes), BF16),
            pltpu.VMEM((slots, probes, points), F32),
            pltpu.VMEM((slots, points, TILE), BF16),
            pltpu.VMEM((slots, points, TILE), BF16),
            pltpu.VMEM((tiles, 1, points), BF16),
            pltpu.VMEM((1, points), BF16),
            pltpu.VMEM((TILE, points), BF16),
            pltpu.VMEM((slots - 1, probes, points), BF16),
            pltpu.VMEM((slots - 1, probes, points), BF16),
            pltpu.VMEM((2, probes, TILE), F32),
            pltpu.VMEM((2, probes, TILE), F32),
            pltpu.VMEM((2, n_col, probes, TILE), F32),
            pltpu.VMEM((2, n_row, probes, TILE), F32),
        ]
        + [dma((len(holders),))] * 2
        + [dma((slots,))] * 4
        + [dma((slots - 1,))] * 2
        + [dma((n_col,)), dma((n_col,)), dma((n_row,)), dma((n_row,))] * 2,
        compiler_params=pltpu.CompilerParams(collective_id=0, has_side_effects=True),
        name="step",
    )(direction, residual, positions, tile_pairs, pair_count)
    square, image_resid = gram[:probes, :probes], gram[:probes, probes : 2 * probes]
    norm_old = gram[probes:, probes : 2 * probes]
    curvature = gram[:probes, 2 * probes : 3 * probes].T
    crossing = gram[probes:, 2 * probes : 3 * probes].T
    step_size = symmetric_solve(curvature, crossing)
    residual_next = residual - apply_left(step_size, applied)
    shifted = jnp.dot(step_size.T, image_resid, precision=HIGHEST)
    quadratic = jnp.dot(
        step_size.T, jnp.dot(square, step_size, precision=HIGHEST), precision=HIGHEST
    )
    norm_new = norm_old - shifted - shifted.T + quadratic
    solution_next = solution_field + apply_left(step_size, direction)
    mix_weight = symmetric_solve(norm_old, norm_new)
    direction_next = residual_next + apply_left(mix_weight, direction)
    return (solution_next, residual_next, direction_next)


def solution(mesh):
    whole = P(None, ("row", "col"))
    return jax.shard_map(
        on_device,
        mesh=mesh,
        in_specs=(whole, whole, whole, whole, whole, P(("row", "col"))),
        out_specs=(whole, whole, whole),
        check_vma=False,
    )
```

```python
import functools
import itertools

import jax
import jax.numpy as jnp
from jax import lax
from jax.experimental import pallas as pl
from jax.experimental.pallas import tpu as pltpu
from jax.sharding import PartitionSpec as P

TILE = 128
BLOCK = 2 * TILE

AMPLITUDE = 0.025
NUGGET = 2.0
SCALE = 4.0
FAR_AWAY = 128.0
HIGHEST = lax.Precision.HIGHEST
MESH = pl.DeviceIdType.MESH
F32 = jnp.float32
BF16 = jnp.bfloat16


def cross_gram_matrix(former, latter):
    return lax.dot_general(
        former, latter, (((1,), (1,)), ((), ())), precision=HIGHEST, preferred_element_type=F32
    )


def apply_left(matrix, vectors):
    return lax.dot_general(
        matrix, vectors, (((0,), (0,)), ((), ())), precision=HIGHEST, preferred_element_type=F32
    )


def eliminate(systems):
    size = systems[0].shape[0]
    row = lax.broadcasted_iota(jnp.int32, systems[0].shape, 0)
    for k in range(size):
        result = []
        for system in systems:
            column = jnp.broadcast_to(system[:, k : k + 1], system.shape)
            scaled = system[k : k + 1] / column[k : k + 1]
            result.append(jnp.where(row == k, scaled, system - column * scaled))
        systems = result
    return systems


def update_kernel(
    gram, applied, solution_field, residual, direction, solution_next, residual_next, direction_next
):
    probes = direction.shape[0]
    sums = gram[...]
    turned = sums.T

    def part(array, row, col):
        return array[row * probes : (row + 1) * probes, col * probes : (col + 1) * probes]

    square, image_resid, norm_old = part(sums, 0, 0), part(sums, 0, 1), part(sums, 1, 1)
    curvature = 0.5 * (part(sums, 0, 2) + part(turned, 2, 0))
    balanced = 0.5 * (norm_old + part(turned, 1, 1))
    eye = [lax.broadcasted_iota(jnp.int32, (probes, probes), axis) for axis in (0, 1)]
    eye = jnp.where(eye[0] == eye[1], 1.0, 0.0)
    fill = jnp.zeros((probes, TILE - 2 * probes), F32)
    first, second = eliminate(
        [
            jnp.concatenate([curvature, part(turned, 2, 1), fill], axis=1),
            jnp.concatenate([balanced, eye, fill], axis=1),
        ]
    )
    step_size, inverse = first[:, probes : 2 * probes], second[:, probes : 2 * probes]
    along = direction[...]
    solution_next[...] = solution_field[...] + apply_left(step_size, along)
    remain = residual[...] - apply_left(step_size, applied[...])
    residual_next[...] = remain
    mixed = jnp.dot(square, step_size, precision=HIGHEST) - image_resid
    norm_new = norm_old + apply_left(step_size, mixed) - apply_left(image_resid, step_size)
    mix_weight = jnp.dot(inverse, norm_new, precision=HIGHEST)
    direction_next[...] = remain + apply_left(mix_weight, along)


@functools.lru_cache(None)
def cover_of(n_row, n_col):
    every = [(r, c) for r in range(n_row) for c in range(n_col)]

    def minus(a, b):
        return ((a[0] - b[0]) % n_row, (a[1] - b[1]) % n_col)

    def cost(e):
        return min(e[0], n_row - e[0]) + min(e[1], n_col - e[1])

    order = sorted(every[1:], key=lambda e: (cost(e), e))
    total = len(every) - 1
    budget = [20000]

    def extend(chosen, seen, start, size):
        if len(chosen) == size:
            return chosen if len(seen) == total else None
        budget[0] -= 1
        rest = size - len(chosen)
        most = sum(2 * (len(chosen) + k) for k in range(rest))
        if budget[0] < 0 or len(seen) + most < total:
            return None
        for k in range(start, len(order)):
            e = order[k]
            new = {minus(e, x) for x in chosen} | {minus(x, e) for x in chosen}
            found = extend(chosen + [e], seen | new, k + 1, size)
            if found:
                return found
        return None

    size = 1
    while size * (size - 1) < total:
        size += 1
    for k in (size, size + 1):
        budget[0] = 20000
        found = extend([(0, 0)], set(), 0, k)
        if found:
            return tuple(found)
    chosen, seen = [(0, 0)], set()
    while len(seen) < total:
        gains = []
        for e in order:
            new = {minus(e, x) for x in chosen} | {minus(x, e) for x in chosen}
            gains.append((-len((new | seen) - {(0, 0)}), cost(e), e))
        e = min(gains)[2]
        seen |= {minus(e, x) for x in chosen} | {minus(x, e) for x in chosen}
        seen.discard((0, 0))
        chosen.append(e)
    return tuple(chosen)


@functools.lru_cache(None)
def units_of(n_row, n_col):
    cover = cover_of(n_row, n_col)
    found = {}
    for i, j in itertools.permutations(range(len(cover)), 2):
        delta = ((cover[j][0] - cover[i][0]) % n_row, (cover[j][1] - cover[i][1]) % n_col)
        found.setdefault(delta, (i, j))
    return tuple(sorted(found.values(), key=lambda u: (max(u), min(u), u)))


def holders_of(n_row, n_col):
    cover = cover_of(n_row, n_col)
    return sorted({(a[0], b[1]) for a in cover for b in cover} - {(0, 0)})


def group_of(n_row, n_col, tiles):
    group = max(1, TILE // (n_row * tiles))
    while n_col % group:
        group -= 1
    return group


def log2(value):
    assert value & (value - 1) == 0
    return value.bit_length() - 1


def pick(index, values):
    result = jnp.int32(values[0])
    for k, value in enumerate(values[1:], 1):
        result = jnp.where(index == k, jnp.int32(value), result)
    return result


class Ring:
    def __init__(self, n_row, n_col):
        self.n_row, self.n_col = n_row, n_col
        self.row, self.col = lax.axis_index("row"), lax.axis_index("col")

    def plus(self, offset):
        return lax.rem(self.row + offset[0], self.n_row), lax.rem(self.col + offset[1], self.n_col)

    def minus(self, offset):
        return self.plus((self.n_row - offset[0], self.n_col - offset[1]))

    def flat(self, place):
        return place[0] * self.n_col + place[1]

    def greet(self):
        barrier = pltpu.get_barrier_semaphore()
        offsets = [(r, c) for r in range(self.n_row) for c in range(self.n_col)][1:]
        for offset in offsets:
            row, col = self.plus(offset)
            pl.semaphore_signal(
                barrier, inc=1, device_id={"row": row, "col": col}, device_id_type=MESH
            )
        pl.semaphore_wait(barrier, len(offsets))


def remote(source, landing, send_sem, recv_sem, place):
    return pltpu.make_async_remote_copy(
        src_ref=source,
        dst_ref=landing,
        send_sem=send_sem,
        recv_sem=recv_sem,
        device_id={"row": place[0], "col": place[1]},
        device_id_type=MESH,
    )


def one_hot(size, index, live=None):
    slots = index.shape[1]
    hit = lax.broadcasted_iota(jnp.int32, (size, slots), 0) == index
    if live is not None:
        hit = hit & live
    return jnp.where(hit, 1.0, 0.0).astype(BF16)


def pattern(ring, tiles, group, tile_pairs, count):
    rows, cols = tile_pairs[0:1, :], tile_pairs[1:2, :]
    live = lax.broadcasted_iota(jnp.int32, rows.shape, 1) < count
    shift, mask = log2(tiles), tiles - 1
    chunk = rows >> shift
    lanes = group * ring.n_row * tiles
    down = ((chunk >> log2(group)) << shift) + (rows & mask)
    across = (chunk & (group - 1)) * (ring.n_row * tiles) + cols
    table = cross_one_hot(one_hot(ring.n_col // group * tiles, down), one_hot(lanes, across, live))
    near, far = rows - ring.col * tiles, cols - ring.row * tiles
    upper = cross_one_hot(one_hot(tiles, near), one_hot(TILE, far, live))
    lower = cross_one_hot(one_hot(tiles, far, live), one_hot(TILE, near))
    eye = lax.broadcasted_iota(jnp.int32, upper.shape, 0) == lax.broadcasted_iota(
        jnp.int32, upper.shape, 1
    )
    return table, upper + lower + jnp.where(eye, 1.0, 0.0)


def cross_one_hot(former, latter):
    return lax.dot_general(former, latter, (((1,), (1,)), ((), ())), preferred_element_type=F32)


def kernel_of(differ_x, differ_y):
    square = (differ_x * differ_x + differ_y * differ_y).astype(F32)
    square = jnp.minimum(jnp.maximum(square, 1e-20), SCALE * SCALE)
    quad = square * lax.rsqrt(square)
    remain = SCALE - quad
    remain = remain * remain
    return (remain * remain * (quad + 1.0)).astype(BF16)


def times_transposed(vectors, block):
    return lax.dot_general(
        vectors, block, (((1,), (1,)), ((), ())), preferred_element_type=F32
    )


def spread_places(slot, places, near_x, near_y):
    pair = places[slot].astype(F32) * SCALE
    points = pair.shape[1]
    side = lax.broadcasted_iota(jnp.int32, (2, 2 * TILE), 1) // TILE
    pick_side = jnp.where(side == lax.broadcasted_iota(jnp.int32, side.shape, 0), 1.0, 0.0)
    both = lax.dot_general(
        pair.astype(BF16),
        pick_side.astype(BF16),
        (((0,), (0,)), ((), ())),
        preferred_element_type=F32,
    ).astype(BF16)
    near_x[slot] = both[:, :TILE]
    near_y[slot] = both[:, TILE:]


def set_far(slot, mask, places, widen, far_x, far_y):
    pair = places[slot].astype(F32) * SCALE
    on = jnp.dot(mask.astype(BF16), widen[...], preferred_element_type=F32)
    x = (pair[0:1] + FAR_AWAY * (1.0 - on)).astype(BF16)
    for a in range(mask.shape[0]):
        far_x[a] = x[a : a + 1]
    far_y[...] = pair[1:2].astype(BF16)


def block_of(slot, base, tile_row, j, near_x, near_y, far_x, far_y):
    rows = []
    for a in range(2):
        at = pl.ds(pl.multiple_of(base + a * TILE, TILE), TILE)
        x, y = near_x[slot, at, :], near_y[slot, at, :]
        row = []
        for b in range(2):
            across = pl.ds(j * BLOCK + b * TILE, TILE)
            row.append(kernel_of(x - far_x[tile_row + a, :, across], y - far_y[:, across]))
        rows.append(jnp.concatenate(row, axis=1))
    return jnp.concatenate(rows, axis=0)


def batches_of(n_row, n_col):
    cover, units = cover_of(n_row, n_col), list(units_of(n_row, n_col))
    result, waited = [], {0}
    for slot in range(1, len(cover)):
        mine = sorted((u for u in units if slot in u), key=lambda u: (sum(u) - slot, u))
        units = [u for u in units if slot not in u]
        cut = [u for u in mine if sum(u) - slot <= len(cover) // 2]
        pieces = [cut, mine[len(cut) :]] if slot == 1 else [mine]
        pieces = [piece for piece in pieces if piece]
        for k, piece in enumerate(pieces):
            need = sorted({s for u in piece for s in u} - waited)
            waited |= set(need)
            result.append((need, piece, slot if k == len(pieces) - 1 else None))
    return result


def step_kernel(
    n_row,
    n_col,
    direction,
    residual,
    positions,
    tile_pairs,
    count,
    applied,
    gram,
    dirs,
    places,
    tables,
    acc,
    near_x,
    near_y,
    far_x,
    far_y,
    widen,
    parts,
    land,
    gram_own,
    gram_half,
    gram_col,
    gram_row,
    *sems,
):
    ring = Ring(n_row, n_col)
    cover, holders = cover_of(n_row, n_col), holders_of(n_row, n_col)
    slots, probes, points = dirs.shape
    tiles, blocks = points // TILE, points // BLOCK
    half = blocks // 2
    group = group_of(n_row, n_col, tiles)
    scale = AMPLITUDE / 256.0
    me = ring.flat((ring.row, ring.col))

    dirs[0] = direction[...].astype(BF16)
    places[0] = positions[...]
    table, own_table = pattern(ring, tiles, group, tile_pairs, count[0])
    tables[me] = table.reshape(tables.shape[1:]).astype(BF16)
    ring.greet()
    sends = []
    for s, offset in enumerate(cover[1:], 1):
        place = ring.minus(offset)
        sends.append(remote(places.at[0], places.at[s], sems[2].at[s], sems[3].at[s], place))
    for k, offset in enumerate(holders):
        place = ring.minus(offset)
        sends.append(remote(tables.at[me], tables.at[me], sems[0].at[k], sems[1].at[k], place))
    for s, offset in enumerate(cover[1:], 1):
        place = ring.minus(offset)
        sends.append(remote(dirs.at[0], dirs.at[s], sems[4].at[s], sems[5].at[s], place))
    for copy in sends:
        copy.start()

    def exchanges(part):
        base = 8 + 4 * part
        over_col = Exchange(
            "col", n_col, gram_own.at[part], gram_col.at[part], sems[base], sems[base + 1]
        )
        over_row = Exchange(
            "row", n_row, gram_half.at[part], gram_row.at[part], sems[base + 2], sems[base + 3]
        )
        return over_col, over_row

    def sum_cols(part):
        total = gram_own[part]
        for k in range(1, n_col):
            total += gram_col[part, lax.rem(ring.col + k, n_col)]
        gram_half[part] = total

    def sum_rows(part):
        total = gram_half[part]
        for k in range(1, n_row):
            total += gram_row[part, lax.rem(ring.row + k, n_row)]
        gram[part * probes : (part + 1) * probes] = total

    def padded(product, before):
        widths = (before, TILE - before - product.shape[1])
        sides = [[jnp.zeros((probes, n), F32)] if n else [] for n in widths]
        return jnp.concatenate(sides[0] + [product] + sides[1], axis=1)

    early_col, early_row = exchanges(1)
    late_col, late_row = exchanges(0)
    sides = jnp.concatenate([residual[...], direction[...]], axis=0)
    gram_own[1] = padded(cross_gram_matrix(residual[...], sides), probes)
    early_col.start()

    acc[...] = jnp.zeros_like(acc)
    lane = lax.broadcasted_iota(jnp.int32, widen.shape, 1) >> log2(TILE)
    widen[...] = jnp.where(lane == lax.broadcasted_iota(jnp.int32, widen.shape, 0), 1.0, 0.0).astype(
        BF16
    )
    spread_places(0, places, near_x, near_y)
    set_far(0, own_table, places, widen, far_x, far_y)

    @pl.loop(0, blocks)
    def _(i):
        base = pl.multiple_of(i * BLOCK, BLOCK)
        total = jnp.zeros((probes, BLOCK), F32)
        for j in range(blocks):
            block = block_of(0, base, 2 * i, j, near_x, near_y, far_x, far_y)
            total += times_transposed(dirs[0, :, j * BLOCK : (j + 1) * BLOCK], block)
        acc[0, :, pl.ds(base, BLOCK)] += total

    for s, offset in enumerate(cover[1:], 1):
        origin = ring.plus(offset)
        remote(places.at[0], places.at[s], sems[2].at[s], sems[3].at[s], origin).wait_recv()

    @pl.loop(1, slots)
    def _(slot):
        spread_places(slot, places, near_x, near_y)

    for k, offset in enumerate(holders):
        origin = ring.plus(offset)
        at = tables.at[ring.flat(origin)]
        remote(at, at, sems[0].at[k], sems[1].at[k], origin).wait_recv()

    rows_of, cols_of = [o[0] for o in cover], [o[1] for o in cover]

    def unit(i, j):
        row_i, col_i = ring.plus((pick(i, rows_of), pick(i, cols_of)))
        row_j, col_j = ring.plus((pick(j, rows_of), pick(j, cols_of)))
        swap = (row_i * n_col + col_i - row_j * n_col - col_j + n_row * n_col) // (n_row * n_col)
        low, high = i + swap * (j - i), j + swap * (i - j)
        row_low = row_i + swap * (row_j - row_i)
        row_high = row_j + swap * (row_i - row_j)
        col_low = col_i + swap * (col_j - col_i)
        col_high = col_j + swap * (col_i - col_j)
        table = tables[row_low * n_col + col_high, col_low // group].astype(F32)
        lanes = table.shape[1]
        start = (col_low % group) * (n_row * tiles) + row_high * tiles
        mask = pltpu.roll(table, lax.rem(lanes - start, lanes), 1)
        set_far(high, mask[:, :TILE], places, widen, far_x, far_y)
        first = swap * half
        forward = [None] * half
        backward = [None] * blocks
        for a in range(half):
            base = pl.multiple_of((first + a) * BLOCK, BLOCK)
            near_vec = dirs[low, :, pl.ds(base, BLOCK)]
            for b in range(blocks):
                block = block_of(low, base, 2 * (first + a), b, near_x, near_y, far_x, far_y)
                ahead = times_transposed(dirs[high, :, b * BLOCK : (b + 1) * BLOCK], block)
                back = jnp.dot(near_vec, block, preferred_element_type=F32)
                forward[a] = ahead if b == 0 else forward[a] + ahead
                backward[b] = back if a == 0 else backward[b] + back
        for a in range(half):
            base = pl.multiple_of((first + a) * BLOCK, BLOCK)
            acc[low, :, pl.ds(base, BLOCK)] += forward[a]
        for b in range(blocks):
            acc[high, :, b * BLOCK : (b + 1) * BLOCK] += backward[b]

    for k, (need, units, complete) in enumerate(batches_of(n_row, n_col)):
        for s in need:
            origin = ring.plus(cover[s])
            remote(dirs.at[0], dirs.at[s], sems[4].at[s], sems[5].at[s], origin).wait_recv()

        @pl.loop(0, len(units))
        def _(t):
            unit(pick(t, [u[0] for u in units]), pick(t, [u[1] for u in units]))

        if k == 0:
            early_col.wait_recv()
            sum_cols(1)
            early_row.start()
        if k == 1:
            early_row.wait_recv()
            sum_rows(1)
        if complete is not None:
            s = complete - 1
            parts[s] = (scale * acc[complete]).astype(BF16)
            copy = remote(
                parts.at[s], land.at[s], sems[6].at[s], sems[7].at[s], ring.plus(cover[complete])
            )
            copy.start()
            sends.append(copy)

    image = scale * acc[0] + NUGGET * direction[...]
    for s, offset in enumerate(cover[1:]):
        origin = ring.minus(offset)
        remote(parts.at[s], land.at[s], sems[6].at[s], sems[7].at[s], origin).wait_recv()
        image += land[s].astype(F32)
    applied[...] = image
    gram_own[0] = padded(cross_gram_matrix(image, jnp.concatenate([image, sides], axis=0)), 0)
    late_col.start()
    late_col.wait_recv()
    sum_cols(0)
    late_row.start()
    late_row.wait_recv()
    sum_rows(0)
    for copy in sends + [early_col, early_row, late_col, late_row]:
        copy.wait_send()


class Exchange:
    def __init__(self, axis, size, source, landing, send_sem, recv_sem):
        self.axis, self.size, self.source, self.landing = axis, size, source, landing
        self.send_sem, self.recv_sem = send_sem, recv_sem
        self.me = lax.axis_index(axis)

    def copy(self, k, source, slot, peer):
        return pltpu.make_async_remote_copy(
            src_ref=source,
            dst_ref=self.landing.at[slot],
            send_sem=self.send_sem.at[k],
            recv_sem=self.recv_sem.at[k],
            device_id={self.axis: peer},
            device_id_type=MESH,
        )

    def outgoing(self, k):
        peer = lax.rem(self.me + k, self.size)
        return self.copy(k, self.source, self.me, peer)

    def start(self):
        for k in range(1, self.size):
            self.outgoing(k).start()

    def wait_recv(self):
        for k in range(1, self.size):
            origin = lax.rem(self.me + self.size - k, self.size)
            self.copy(k, self.landing.at[origin], origin, origin).wait_recv()

    def wait_send(self):
        for k in range(1, self.size):
            self.outgoing(k).wait_send()


def on_device(solution_field, residual, direction, positions, tile_pairs, pair_count):
    probes, points = direction.shape
    n_row, n_col = lax.axis_size("row"), lax.axis_size("col")
    cover, holders = cover_of(n_row, n_col), holders_of(n_row, n_col)
    slots, tiles = len(cover), points // TILE
    group = group_of(n_row, n_col, tiles)
    lanes = group * n_row * tiles
    vmem = pl.BlockSpec(memory_space=pltpu.VMEM)
    smem = pl.BlockSpec(memory_space=pltpu.SMEM)
    dma = pltpu.SemaphoreType.DMA
    applied, gram = pl.pallas_call(
        functools.partial(step_kernel, n_row, n_col),
        out_shape=(
            jax.ShapeDtypeStruct((probes, points), F32),
            jax.ShapeDtypeStruct((2 * probes, TILE), F32),
        ),
        in_specs=[vmem] * 4 + [smem],
        out_specs=(vmem, vmem),
        scratch_shapes=[
            pltpu.VMEM((slots, probes, points), BF16),
            pltpu.VMEM((slots, 2, points), BF16),
            pltpu.VMEM((n_row * n_col, n_col // group, tiles, lanes), BF16),
            pltpu.VMEM((slots, probes, points), F32),
            pltpu.VMEM((slots, points, TILE), BF16),
            pltpu.VMEM((slots, points, TILE), BF16),
            pltpu.VMEM((tiles, 1, points), BF16),
            pltpu.VMEM((1, points), BF16),
            pltpu.VMEM((TILE, points), BF16),
            pltpu.VMEM((slots - 1, probes, points), BF16),
            pltpu.VMEM((slots - 1, probes, points), BF16),
            pltpu.VMEM((2, probes, TILE), F32),
            pltpu.VMEM((2, probes, TILE), F32),
            pltpu.VMEM((2, n_col, probes, TILE), F32),
            pltpu.VMEM((2, n_row, probes, TILE), F32),
        ]
        + [dma((len(holders),))] * 2
        + [dma((slots,))] * 4
        + [dma((slots - 1,))] * 2
        + [dma((n_col,)), dma((n_col,)), dma((n_row,)), dma((n_row,))] * 2,
        compiler_params=pltpu.CompilerParams(collective_id=0, has_side_effects=True),
        name="step",
    )(direction, residual, positions, tile_pairs, pair_count)
    return pl.pallas_call(
        update_kernel,
        out_shape=(jax.ShapeDtypeStruct((probes, points), F32),) * 3,
        in_specs=[vmem] * 5,
        out_specs=(vmem,) * 3,
        name="update",
    )(gram, applied, solution_field, residual, direction)


def solution(mesh):
    whole = P(None, ("row", "col"))
    return jax.shard_map(
        on_device,
        mesh=mesh,
        in_specs=(whole, whole, whole, whole, whole, P(("row", "col"))),
        out_specs=(whole, whole, whole),
        check_vma=False,
    )
```

```python
import functools
import itertools

import jax
import jax.numpy as jnp
from jax import lax
from jax.experimental import pallas as pl
from jax.experimental.pallas import tpu as pltpu
from jax.sharding import PartitionSpec as P

TILE = 128
BLOCK = 2 * TILE

AMPLITUDE = 0.025
NUGGET = 2.0
SCALE = 4.0
FAR_AWAY = 128.0
HIGHEST = lax.Precision.HIGHEST
MESH = pl.DeviceIdType.MESH
F32 = jnp.float32
BF16 = jnp.bfloat16


def cross_gram_matrix(former, latter):
    return lax.dot_general(
        former, latter, (((1,), (1,)), ((), ())), precision=HIGHEST, preferred_element_type=F32
    )


def apply_left(matrix, vectors):
    return lax.dot_general(
        matrix, vectors, (((0,), (0,)), ((), ())), precision=HIGHEST, preferred_element_type=F32
    )


def eliminate(systems):
    size = systems[0].shape[0]
    row = lax.broadcasted_iota(jnp.int32, systems[0].shape, 0)
    for k in range(size):
        result = []
        for system in systems:
            column = jnp.broadcast_to(system[:, k : k + 1], system.shape)
            scaled = system[k : k + 1] / column[k : k + 1]
            result.append(jnp.where(row == k, scaled, system - column * scaled))
        systems = result
    return systems


def update_kernel(
    gram, applied, solution_field, residual, direction, solution_next, residual_next, direction_next
):
    probes = direction.shape[0]
    sums = gram[...]
    turned = sums.T

    def part(array, row, col):
        return array[row * probes : (row + 1) * probes, col * probes : (col + 1) * probes]

    square, image_resid, norm_old = part(sums, 0, 0), part(sums, 0, 1), part(sums, 1, 1)
    curvature = 0.5 * (part(sums, 0, 2) + part(turned, 2, 0))
    balanced = 0.5 * (norm_old + part(turned, 1, 1))
    eye = [lax.broadcasted_iota(jnp.int32, (probes, probes), axis) for axis in (0, 1)]
    eye = jnp.where(eye[0] == eye[1], 1.0, 0.0)
    fill = jnp.zeros((probes, TILE - 2 * probes), F32)
    first, second = eliminate(
        [
            jnp.concatenate([curvature, part(turned, 2, 1), fill], axis=1),
            jnp.concatenate([balanced, eye, fill], axis=1),
        ]
    )
    step_size, inverse = first[:, probes : 2 * probes], second[:, probes : 2 * probes]
    along = direction[...]
    solution_next[...] = solution_field[...] + apply_left(step_size, along)
    remain = residual[...] - apply_left(step_size, applied[...])
    residual_next[...] = remain
    mixed = jnp.dot(square, step_size, precision=HIGHEST) - image_resid
    norm_new = norm_old + apply_left(step_size, mixed) - apply_left(image_resid, step_size)
    mix_weight = jnp.dot(inverse, norm_new, precision=HIGHEST)
    direction_next[...] = remain + apply_left(mix_weight, along)


@functools.lru_cache(None)
def cover_of(n_row, n_col):
    every = [(r, c) for r in range(n_row) for c in range(n_col)]

    def minus(a, b):
        return ((a[0] - b[0]) % n_row, (a[1] - b[1]) % n_col)

    def cost(e):
        return min(e[0], n_row - e[0]) + min(e[1], n_col - e[1])

    order = sorted(every[1:], key=lambda e: (cost(e), e))
    total = len(every) - 1
    budget = [20000]

    def extend(chosen, seen, start, size):
        if len(chosen) == size:
            return chosen if len(seen) == total else None
        budget[0] -= 1
        rest = size - len(chosen)
        most = sum(2 * (len(chosen) + k) for k in range(rest))
        if budget[0] < 0 or len(seen) + most < total:
            return None
        for k in range(start, len(order)):
            e = order[k]
            new = {minus(e, x) for x in chosen} | {minus(x, e) for x in chosen}
            found = extend(chosen + [e], seen | new, k + 1, size)
            if found:
                return found
        return None

    size = 1
    while size * (size - 1) < total:
        size += 1
    for k in (size, size + 1):
        budget[0] = 20000
        found = extend([(0, 0)], set(), 0, k)
        if found:
            return tuple(found)
    chosen, seen = [(0, 0)], set()
    while len(seen) < total:
        gains = []
        for e in order:
            new = {minus(e, x) for x in chosen} | {minus(x, e) for x in chosen}
            gains.append((-len((new | seen) - {(0, 0)}), cost(e), e))
        e = min(gains)[2]
        seen |= {minus(e, x) for x in chosen} | {minus(x, e) for x in chosen}
        seen.discard((0, 0))
        chosen.append(e)
    return tuple(chosen)


@functools.lru_cache(None)
def units_of(n_row, n_col):
    cover = cover_of(n_row, n_col)
    found = {}
    for i, j in itertools.permutations(range(len(cover)), 2):
        delta = ((cover[j][0] - cover[i][0]) % n_row, (cover[j][1] - cover[i][1]) % n_col)
        found.setdefault(delta, (i, j))
    return tuple(sorted(found.values(), key=lambda u: (max(u), min(u), u)))


def holders_of(n_row, n_col):
    cover = cover_of(n_row, n_col)
    return sorted({(a[0], b[1]) for a in cover for b in cover} - {(0, 0)})


def group_of(n_row, n_col, tiles):
    group = max(1, TILE // (n_row * tiles))
    while n_col % group:
        group -= 1
    return group


def log2(value):
    assert value & (value - 1) == 0
    return value.bit_length() - 1


def pick(index, values):
    result = jnp.int32(values[0])
    for k, value in enumerate(values[1:], 1):
        result = jnp.where(index == k, jnp.int32(value), result)
    return result


class Ring:
    def __init__(self, n_row, n_col):
        self.n_row, self.n_col = n_row, n_col
        self.row, self.col = lax.axis_index("row"), lax.axis_index("col")

    def plus(self, offset):
        return lax.rem(self.row + offset[0], self.n_row), lax.rem(self.col + offset[1], self.n_col)

    def minus(self, offset):
        return self.plus((self.n_row - offset[0], self.n_col - offset[1]))

    def flat(self, place):
        return place[0] * self.n_col + place[1]

    def greet(self):
        offsets = [(r, c) for r in range(self.n_row) for c in range(self.n_col)][1:]
        for offset in offsets:
            row, col = self.plus(offset)
            pl.semaphore_signal(
                pltpu.get_barrier_semaphore(),
                inc=1,
                device_id={"row": row, "col": col},
                device_id_type=MESH,
            )

    def wait_greeted(self):
        pl.semaphore_wait(pltpu.get_barrier_semaphore(), self.n_row * self.n_col - 1)


def remote(source, landing, send_sem, recv_sem, place):
    return pltpu.make_async_remote_copy(
        src_ref=source,
        dst_ref=landing,
        send_sem=send_sem,
        recv_sem=recv_sem,
        device_id={"row": place[0], "col": place[1]},
        device_id_type=MESH,
    )


def one_hot(size, index, live=None):
    slots = index.shape[1]
    hit = lax.broadcasted_iota(jnp.int32, (size, slots), 0) == index
    if live is not None:
        hit = hit & live
    return jnp.where(hit, 1.0, 0.0).astype(BF16)


def pattern(ring, tiles, group, tile_pairs, count):
    rows, cols = tile_pairs[0:1, :], tile_pairs[1:2, :]
    live = lax.broadcasted_iota(jnp.int32, rows.shape, 1) < count
    shift, mask = log2(tiles), tiles - 1
    chunk = rows >> shift
    lanes = group * ring.n_row * tiles
    down = ((chunk >> log2(group)) << shift) + (rows & mask)
    across = (chunk & (group - 1)) * (ring.n_row * tiles) + cols
    table = cross_one_hot(one_hot(ring.n_col // group * tiles, down), one_hot(lanes, across, live))
    near, far = rows - ring.col * tiles, cols - ring.row * tiles
    upper = cross_one_hot(one_hot(tiles, near), one_hot(TILE, far, live))
    lower = cross_one_hot(one_hot(tiles, far, live), one_hot(TILE, near))
    eye = lax.broadcasted_iota(jnp.int32, upper.shape, 0) == lax.broadcasted_iota(
        jnp.int32, upper.shape, 1
    )
    return table, upper + lower + jnp.where(eye, 1.0, 0.0)


def cross_one_hot(former, latter):
    return lax.dot_general(former, latter, (((1,), (1,)), ((), ())), preferred_element_type=F32)


def kernel_of(differ_x, differ_y):
    square = differ_x * differ_x + differ_y * differ_y
    square = jnp.minimum(jnp.maximum(square, BF16(1e-20)), BF16(SCALE * SCALE)).astype(F32)
    quad = square * lax.rsqrt(square)
    remain = SCALE - quad
    remain = remain * remain
    return (remain * remain * (quad + 1.0)).astype(BF16)


def times_transposed(vectors, block):
    return lax.dot_general(
        vectors, block, (((1,), (1,)), ((), ())), preferred_element_type=F32
    )


def spread_places(slot, places, near_x, near_y):
    pair = places[slot].astype(F32) * SCALE
    points = pair.shape[1]
    side = lax.broadcasted_iota(jnp.int32, (2, 2 * TILE), 1) // TILE
    pick_side = jnp.where(side == lax.broadcasted_iota(jnp.int32, side.shape, 0), 1.0, 0.0)
    both = lax.dot_general(
        pair.astype(BF16),
        pick_side.astype(BF16),
        (((0,), (0,)), ((), ())),
        preferred_element_type=F32,
    ).astype(BF16)
    near_x[slot] = both[:, :TILE]
    near_y[slot] = both[:, TILE:]


def set_far(slot, mask, places, widen, far_x, far_y):
    pair = places[slot].astype(F32) * SCALE
    on = jnp.dot(mask.astype(BF16), widen[...], preferred_element_type=F32)
    x = (pair[0:1] + FAR_AWAY * (1.0 - on)).astype(BF16)
    for a in range(mask.shape[0]):
        far_x[a] = x[a : a + 1]
    far_y[...] = pair[1:2].astype(BF16)


def block_of(slot, base, tile_row, j, near_x, near_y, far_x, far_y):
    rows = []
    for a in range(2):
        at = pl.ds(pl.multiple_of(base + a * TILE, TILE), TILE)
        x, y = near_x[slot, at, :], near_y[slot, at, :]
        row = []
        for b in range(2):
            across = pl.ds(j * BLOCK + b * TILE, TILE)
            row.append(kernel_of(x - far_x[tile_row + a, :, across], y - far_y[:, across]))
        rows.append(jnp.concatenate(row, axis=1))
    return jnp.concatenate(rows, axis=0)


def batches_of(n_row, n_col):
    cover, units = cover_of(n_row, n_col), list(units_of(n_row, n_col))
    start = len(cover) // 2
    order = [start] + [s for s in range(len(cover) - 1, 0, -1) if s != start]
    result, waited = [], {0}
    for slot in order:
        mine = sorted((u for u in units if slot in u), key=lambda u: (sum(u) - slot, u))
        units = [u for u in units if slot not in u]
        cut = [u for u in mine if sum(u) - slot < start]
        pieces = [cut, mine[len(cut) :]] if slot == start else [mine]
        pieces = [piece for piece in pieces if piece]
        for k, piece in enumerate(pieces):
            need = sorted({s for u in piece for s in u} - waited)
            waited |= set(need)
            result.append((need, piece, slot if k == len(pieces) - 1 else None))
    return result


def step_kernel(
    n_row,
    n_col,
    direction,
    residual,
    positions,
    tile_pairs,
    count,
    applied,
    gram,
    dirs,
    places,
    tables,
    acc,
    near_x,
    near_y,
    far_x,
    far_y,
    widen,
    parts,
    land,
    gram_own,
    gram_half,
    gram_col,
    gram_row,
    *sems,
):
    ring = Ring(n_row, n_col)
    cover, holders = cover_of(n_row, n_col), holders_of(n_row, n_col)
    slots, probes, points = dirs.shape
    tiles, blocks = points // TILE, points // BLOCK
    half = blocks // 2
    group = group_of(n_row, n_col, tiles)
    scale = AMPLITUDE / 256.0
    me = ring.flat((ring.row, ring.col))

    ring.greet()
    dirs[0] = direction[...].astype(BF16)
    places[0] = positions[...]
    table, own_table = pattern(ring, tiles, group, tile_pairs, count[0])
    tables[me] = table.reshape(tables.shape[1:]).astype(BF16)
    ring.wait_greeted()
    sends = []
    for s, offset in enumerate(cover[1:], 1):
        place = ring.minus(offset)
        sends.append(remote(places.at[0], places.at[s], sems[2].at[s], sems[3].at[s], place))
    for k, offset in enumerate(holders):
        place = ring.minus(offset)
        sends.append(remote(tables.at[me], tables.at[me], sems[0].at[k], sems[1].at[k], place))
    for s, offset in enumerate(cover[1:], 1):
        place = ring.minus(offset)
        sends.append(remote(dirs.at[0], dirs.at[s], sems[4].at[s], sems[5].at[s], place))
    for copy in sends:
        copy.start()

    def exchanges(part):
        base = 8 + 4 * part
        over_col = Exchange(
            "col", n_col, gram_own.at[part], gram_col.at[part], sems[base], sems[base + 1]
        )
        over_row = Exchange(
            "row", n_row, gram_half.at[part], gram_row.at[part], sems[base + 2], sems[base + 3]
        )
        return over_col, over_row

    def sum_cols(part):
        total = gram_own[part]
        for k in range(1, n_col):
            total += gram_col[part, lax.rem(ring.col + k, n_col)]
        gram_half[part] = total

    def sum_rows(part):
        total = gram_half[part]
        for k in range(1, n_row):
            total += gram_row[part, lax.rem(ring.row + k, n_row)]
        gram[part * probes : (part + 1) * probes] = total

    def padded(product, before):
        widths = (before, TILE - before - product.shape[1])
        sides = [[jnp.zeros((probes, n), F32)] if n else [] for n in widths]
        return jnp.concatenate(sides[0] + [product] + sides[1], axis=1)

    early_col, early_row = exchanges(1)
    late_col, late_row = exchanges(0)
    sides = jnp.concatenate([residual[...], direction[...]], axis=0)
    gram_own[1] = padded(cross_gram_matrix(residual[...], sides), probes)
    early_col.start()

    acc[...] = jnp.zeros_like(acc)
    lane = lax.broadcasted_iota(jnp.int32, widen.shape, 1) >> log2(TILE)
    widen[...] = jnp.where(lane == lax.broadcasted_iota(jnp.int32, widen.shape, 0), 1.0, 0.0).astype(
        BF16
    )
    spread_places(0, places, near_x, near_y)
    set_far(0, own_table, places, widen, far_x, far_y)

    @pl.loop(0, blocks)
    def _(i):
        base = pl.multiple_of(i * BLOCK, BLOCK)
        total = jnp.zeros((probes, BLOCK), F32)
        for j in range(blocks):
            block = block_of(0, base, 2 * i, j, near_x, near_y, far_x, far_y)
            total += times_transposed(dirs[0, :, j * BLOCK : (j + 1) * BLOCK], block)
        acc[0, :, pl.ds(base, BLOCK)] += total

    for s, offset in enumerate(cover[1:], 1):
        origin = ring.plus(offset)
        remote(places.at[0], places.at[s], sems[2].at[s], sems[3].at[s], origin).wait_recv()

    @pl.loop(1, slots)
    def _(slot):
        spread_places(slot, places, near_x, near_y)

    for k, offset in enumerate(holders):
        origin = ring.plus(offset)
        at = tables.at[ring.flat(origin)]
        remote(at, at, sems[0].at[k], sems[1].at[k], origin).wait_recv()

    rows_of, cols_of = [o[0] for o in cover], [o[1] for o in cover]

    def prepare(i, j):
        row_i, col_i = ring.plus((pick(i, rows_of), pick(i, cols_of)))
        row_j, col_j = ring.plus((pick(j, rows_of), pick(j, cols_of)))
        swap = (row_i * n_col + col_i - row_j * n_col - col_j + n_row * n_col) // (n_row * n_col)
        low, high = i + swap * (j - i), j + swap * (i - j)
        row_low = row_i + swap * (row_j - row_i)
        row_high = row_j + swap * (row_i - row_j)
        col_low = col_i + swap * (col_j - col_i)
        col_high = col_j + swap * (col_i - col_j)
        table = tables[row_low * n_col + col_high, col_low // group].astype(F32)
        lanes = table.shape[1]
        start = (col_low % group) * (n_row * tiles) + row_high * tiles
        mask = pltpu.roll(table, lax.rem(lanes - start, lanes), 1)
        set_far(high, mask[:, :TILE], places, widen, far_x, far_y)
        return low, high, swap * half

    def unit(low, high, first):
        forward = [None] * half
        backward = [None] * blocks
        for a in range(half):
            base = pl.multiple_of((first + a) * BLOCK, BLOCK)
            near_vec = dirs[low, :, pl.ds(base, BLOCK)]
            for b in range(blocks):
                block = block_of(low, base, 2 * (first + a), b, near_x, near_y, far_x, far_y)
                ahead = times_transposed(dirs[high, :, b * BLOCK : (b + 1) * BLOCK], block)
                back = jnp.dot(near_vec, block, preferred_element_type=F32)
                forward[a] = ahead if b == 0 else forward[a] + ahead
                backward[b] = back if a == 0 else backward[b] + back
        for a in range(half):
            base = pl.multiple_of((first + a) * BLOCK, BLOCK)
            acc[low, :, pl.ds(base, BLOCK)] += forward[a]
        for b in range(blocks):
            acc[high, :, b * BLOCK : (b + 1) * BLOCK] += backward[b]

    batches = batches_of(n_row, n_col)
    every = [u for _, units, _ in batches for u in units]
    state = prepare(jnp.int32(every[0][0]), jnp.int32(every[0][1]))
    done = 0
    for k, (need, units, complete) in enumerate(batches):
        for s in need:
            origin = ring.plus(cover[s])
            remote(dirs.at[0], dirs.at[s], sems[4].at[s], sems[5].at[s], origin).wait_recv()
        done += len(units)
        coming = units[1:] + [every[done % len(every)]]

        def one(t, now):
            unit(*now)
            return prepare(pick(t, [u[0] for u in coming]), pick(t, [u[1] for u in coming]))

        state = lax.fori_loop(0, len(units), one, state)

        if k == 0:
            early_col.wait_recv()
            sum_cols(1)
            early_row.start()
        if k == 1:
            early_row.wait_recv()
            sum_rows(1)
        if complete is not None:
            s = complete - 1
            parts[s] = (scale * acc[complete]).astype(BF16)
            copy = remote(
                parts.at[s], land.at[s], sems[6].at[s], sems[7].at[s], ring.plus(cover[complete])
            )
            copy.start()
            sends.append(copy)

    image = scale * acc[0] + NUGGET * direction[...]
    for s, offset in enumerate(cover[1:]):
        origin = ring.minus(offset)
        remote(parts.at[s], land.at[s], sems[6].at[s], sems[7].at[s], origin).wait_recv()
        image += land[s].astype(F32)
    applied[...] = image
    gram_own[0] = padded(cross_gram_matrix(image, jnp.concatenate([image, sides], axis=0)), 0)
    late_col.start()
    late_col.wait_recv()
    sum_cols(0)
    late_row.start()
    late_row.wait_recv()
    sum_rows(0)
    for copy in sends + [early_col, early_row, late_col, late_row]:
        copy.wait_send()


class Exchange:
    def __init__(self, axis, size, source, landing, send_sem, recv_sem):
        self.axis, self.size, self.source, self.landing = axis, size, source, landing
        self.send_sem, self.recv_sem = send_sem, recv_sem
        self.me = lax.axis_index(axis)

    def copy(self, k, source, slot, peer):
        return pltpu.make_async_remote_copy(
            src_ref=source,
            dst_ref=self.landing.at[slot],
            send_sem=self.send_sem.at[k],
            recv_sem=self.recv_sem.at[k],
            device_id={self.axis: peer},
            device_id_type=MESH,
        )

    def outgoing(self, k):
        peer = lax.rem(self.me + k, self.size)
        return self.copy(k, self.source, self.me, peer)

    def start(self):
        for k in range(1, self.size):
            self.outgoing(k).start()

    def wait_recv(self):
        for k in range(1, self.size):
            origin = lax.rem(self.me + self.size - k, self.size)
            self.copy(k, self.landing.at[origin], origin, origin).wait_recv()

    def wait_send(self):
        for k in range(1, self.size):
            self.outgoing(k).wait_send()


def on_device(solution_field, residual, direction, positions, tile_pairs, pair_count):
    probes, points = direction.shape
    n_row, n_col = lax.axis_size("row"), lax.axis_size("col")
    cover, holders = cover_of(n_row, n_col), holders_of(n_row, n_col)
    slots, tiles = len(cover), points // TILE
    group = group_of(n_row, n_col, tiles)
    lanes = group * n_row * tiles
    vmem = pl.BlockSpec(memory_space=pltpu.VMEM)
    smem = pl.BlockSpec(memory_space=pltpu.SMEM)
    dma = pltpu.SemaphoreType.DMA
    applied, gram = pl.pallas_call(
        functools.partial(step_kernel, n_row, n_col),
        out_shape=(
            jax.ShapeDtypeStruct((probes, points), F32),
            jax.ShapeDtypeStruct((2 * probes, TILE), F32),
        ),
        in_specs=[vmem] * 4 + [smem],
        out_specs=(vmem, vmem),
        scratch_shapes=[
            pltpu.VMEM((slots, probes, points), BF16),
            pltpu.VMEM((slots, 2, points), BF16),
            pltpu.VMEM((n_row * n_col, n_col // group, tiles, lanes), BF16),
            pltpu.VMEM((slots, probes, points), F32),
            pltpu.VMEM((slots, points, TILE), BF16),
            pltpu.VMEM((slots, points, TILE), BF16),
            pltpu.VMEM((tiles, 1, points), BF16),
            pltpu.VMEM((1, points), BF16),
            pltpu.VMEM((TILE, points), BF16),
            pltpu.VMEM((slots - 1, probes, points), BF16),
            pltpu.VMEM((slots - 1, probes, points), BF16),
            pltpu.VMEM((2, probes, TILE), F32),
            pltpu.VMEM((2, probes, TILE), F32),
            pltpu.VMEM((2, n_col, probes, TILE), F32),
            pltpu.VMEM((2, n_row, probes, TILE), F32),
        ]
        + [dma((len(holders),))] * 2
        + [dma((slots,))] * 4
        + [dma((slots - 1,))] * 2
        + [dma((n_col,)), dma((n_col,)), dma((n_row,)), dma((n_row,))] * 2,
        compiler_params=pltpu.CompilerParams(collective_id=0, has_side_effects=True),
        name="step",
    )(direction, residual, positions, tile_pairs, pair_count)
    return pl.pallas_call(
        update_kernel,
        out_shape=(jax.ShapeDtypeStruct((probes, points), F32),) * 3,
        in_specs=[vmem] * 5,
        out_specs=(vmem,) * 3,
        name="update",
    )(gram, applied, solution_field, residual, direction)


def solution(mesh):
    whole = P(None, ("row", "col"))
    return jax.shard_map(
        on_device,
        mesh=mesh,
        in_specs=(whole, whole, whole, whole, whole, P(("row", "col"))),
        out_specs=(whole, whole, whole),
        check_vma=False,
    )
```

```python
import functools
import itertools

import jax
import jax.numpy as jnp
from jax import lax
from jax.experimental import pallas as pl
from jax.experimental.pallas import tpu as pltpu
from jax.sharding import PartitionSpec as P

TILE = 128
BLOCK = 2 * TILE

AMPLITUDE = 0.025
NUGGET = 2.0
SCALE = 4.0
FAR_AWAY = 128.0
HIGHEST = lax.Precision.HIGHEST
MESH = pl.DeviceIdType.MESH
F32 = jnp.float32
BF16 = jnp.bfloat16


def cross_gram_matrix(former, latter):
    return lax.dot_general(
        former, latter, (((1,), (1,)), ((), ())), precision=HIGHEST, preferred_element_type=F32
    )


def apply_left(matrix, vectors):
    return lax.dot_general(
        matrix, vectors, (((0,), (0,)), ((), ())), precision=HIGHEST, preferred_element_type=F32
    )


def eliminate(systems):
    size = systems[0].shape[0]
    row = lax.broadcasted_iota(jnp.int32, systems[0].shape, 0)
    for k in range(size):
        result = []
        for system in systems:
            column = jnp.broadcast_to(system[:, k : k + 1], system.shape)
            scaled = system[k : k + 1] / column[k : k + 1]
            result.append(jnp.where(row == k, scaled, system - column * scaled))
        systems = result
    return systems


def update_kernel(
    gram, applied, solution_field, residual, direction, solution_next, residual_next, direction_next
):
    probes = direction.shape[0]
    sums = gram[...]
    turned = sums.T

    def part(array, row, col):
        return array[row * probes : (row + 1) * probes, col * probes : (col + 1) * probes]

    square, image_resid, norm_old = part(sums, 0, 0), part(sums, 0, 1), part(sums, 1, 1)
    curvature = 0.5 * (part(sums, 0, 2) + part(turned, 2, 0))
    balanced = 0.5 * (norm_old + part(turned, 1, 1))
    eye = [lax.broadcasted_iota(jnp.int32, (probes, probes), axis) for axis in (0, 1)]
    eye = jnp.where(eye[0] == eye[1], 1.0, 0.0)
    fill = jnp.zeros((probes, TILE - 2 * probes), F32)
    first, second = eliminate(
        [
            jnp.concatenate([curvature, part(turned, 2, 1), fill], axis=1),
            jnp.concatenate([balanced, eye, fill], axis=1),
        ]
    )
    step_size, inverse = first[:, probes : 2 * probes], second[:, probes : 2 * probes]
    along = direction[...]
    solution_next[...] = solution_field[...] + apply_left(step_size, along)
    remain = residual[...] - apply_left(step_size, applied[...])
    residual_next[...] = remain
    mixed = jnp.dot(square, step_size, precision=HIGHEST) - image_resid
    norm_new = norm_old + apply_left(step_size, mixed) - apply_left(image_resid, step_size)
    mix_weight = jnp.dot(inverse, norm_new, precision=HIGHEST)
    direction_next[...] = remain + apply_left(mix_weight, along)


@functools.lru_cache(None)
def cover_of(n_row, n_col):
    every = [(r, c) for r in range(n_row) for c in range(n_col)]

    def minus(a, b):
        return ((a[0] - b[0]) % n_row, (a[1] - b[1]) % n_col)

    def cost(e):
        return min(e[0], n_row - e[0]) + min(e[1], n_col - e[1])

    order = sorted(every[1:], key=lambda e: (cost(e), e))
    total = len(every) - 1
    budget = [20000]

    def extend(chosen, seen, start, size):
        if len(chosen) == size:
            return chosen if len(seen) == total else None
        budget[0] -= 1
        rest = size - len(chosen)
        most = sum(2 * (len(chosen) + k) for k in range(rest))
        if budget[0] < 0 or len(seen) + most < total:
            return None
        for k in range(start, len(order)):
            e = order[k]
            new = {minus(e, x) for x in chosen} | {minus(x, e) for x in chosen}
            found = extend(chosen + [e], seen | new, k + 1, size)
            if found:
                return found
        return None

    size = 1
    while size * (size - 1) < total:
        size += 1
    for k in (size, size + 1):
        budget[0] = 20000
        found = extend([(0, 0)], set(), 0, k)
        if found:
            return tuple(found)
    chosen, seen = [(0, 0)], set()
    while len(seen) < total:
        gains = []
        for e in order:
            new = {minus(e, x) for x in chosen} | {minus(x, e) for x in chosen}
            gains.append((-len((new | seen) - {(0, 0)}), cost(e), e))
        e = min(gains)[2]
        seen |= {minus(e, x) for x in chosen} | {minus(x, e) for x in chosen}
        seen.discard((0, 0))
        chosen.append(e)
    return tuple(chosen)


@functools.lru_cache(None)
def units_of(n_row, n_col):
    cover = cover_of(n_row, n_col)
    found = {}
    for i, j in itertools.permutations(range(len(cover)), 2):
        delta = ((cover[j][0] - cover[i][0]) % n_row, (cover[j][1] - cover[i][1]) % n_col)
        found.setdefault(delta, (i, j))
    return tuple(sorted(found.values(), key=lambda u: (max(u), min(u), u)))


def holders_of(n_row, n_col):
    cover = cover_of(n_row, n_col)
    return sorted({(a[0], b[1]) for a in cover for b in cover} - {(0, 0)})


def group_of(n_row, n_col, tiles):
    group = max(1, TILE // (n_row * tiles))
    while n_col % group:
        group -= 1
    return group


def log2(value):
    assert value & (value - 1) == 0
    return value.bit_length() - 1


def pick(index, values):
    result = jnp.int32(values[0])
    for k, value in enumerate(values[1:], 1):
        result = jnp.where(index == k, jnp.int32(value), result)
    return result


class Ring:
    def __init__(self, n_row, n_col):
        self.n_row, self.n_col = n_row, n_col
        self.row, self.col = lax.axis_index("row"), lax.axis_index("col")

    def plus(self, offset):
        return lax.rem(self.row + offset[0], self.n_row), lax.rem(self.col + offset[1], self.n_col)

    def minus(self, offset):
        return self.plus((self.n_row - offset[0], self.n_col - offset[1]))

    def flat(self, place):
        return place[0] * self.n_col + place[1]

    def greet(self):
        offsets = [(r, c) for r in range(self.n_row) for c in range(self.n_col)][1:]
        for offset in offsets:
            row, col = self.plus(offset)
            pl.semaphore_signal(
                pltpu.get_barrier_semaphore(),
                inc=1,
                device_id={"row": row, "col": col},
                device_id_type=MESH,
            )

    def wait_greeted(self):
        pl.semaphore_wait(pltpu.get_barrier_semaphore(), self.n_row * self.n_col - 1)


def remote(source, landing, send_sem, recv_sem, place):
    return pltpu.make_async_remote_copy(
        src_ref=source,
        dst_ref=landing,
        send_sem=send_sem,
        recv_sem=recv_sem,
        device_id={"row": place[0], "col": place[1]},
        device_id_type=MESH,
    )


def one_hot(size, index, live=None):
    slots = index.shape[1]
    hit = lax.broadcasted_iota(jnp.int32, (size, slots), 0) == index
    if live is not None:
        hit = hit & live
    return jnp.where(hit, 1.0, 0.0).astype(BF16)


def pattern(ring, tiles, group, tile_pairs, count):
    rows, cols = tile_pairs[0:1, :], tile_pairs[1:2, :]
    live = lax.broadcasted_iota(jnp.int32, rows.shape, 1) < count
    shift, mask = log2(tiles), tiles - 1
    chunk = rows >> shift
    lanes = group * ring.n_row * tiles
    down = ((chunk >> log2(group)) << shift) + (rows & mask)
    across = (chunk & (group - 1)) * (ring.n_row * tiles) + cols
    table = cross_one_hot(one_hot(ring.n_col // group * tiles, down), one_hot(lanes, across, live))
    near, far = rows - ring.col * tiles, cols - ring.row * tiles
    upper = cross_one_hot(one_hot(tiles, near), one_hot(TILE, far, live))
    lower = cross_one_hot(one_hot(tiles, far, live), one_hot(TILE, near))
    eye = lax.broadcasted_iota(jnp.int32, upper.shape, 0) == lax.broadcasted_iota(
        jnp.int32, upper.shape, 1
    )
    return table, upper + lower + jnp.where(eye, 1.0, 0.0)


def cross_one_hot(former, latter):
    return lax.dot_general(former, latter, (((1,), (1,)), ((), ())), preferred_element_type=F32)


def kernel_of(differ_x, differ_y):
    square = differ_x * differ_x + differ_y * differ_y
    square = jnp.minimum(jnp.maximum(square, BF16(1e-20)), BF16(SCALE * SCALE)).astype(F32)
    quad = square * lax.rsqrt(square)
    remain = SCALE - quad
    remain = remain * remain
    return (remain * remain * (quad + 1.0)).astype(BF16)


def times_transposed(vectors, block):
    return lax.dot_general(
        vectors, block, (((1,), (1,)), ((), ())), preferred_element_type=F32
    )


def spread_places(slot, places, near_x, near_y):
    pair = places[slot].astype(F32) * SCALE
    points = pair.shape[1]
    side = lax.broadcasted_iota(jnp.int32, (2, 2 * TILE), 1) // TILE
    pick_side = jnp.where(side == lax.broadcasted_iota(jnp.int32, side.shape, 0), 1.0, 0.0)
    both = lax.dot_general(
        pair.astype(BF16),
        pick_side.astype(BF16),
        (((0,), (0,)), ((), ())),
        preferred_element_type=F32,
    ).astype(BF16)
    near_x[slot] = both[:, :TILE]
    near_y[slot] = both[:, TILE:]


def set_far(slot, mask, places, widen, far_x, far_y):
    pair = places[slot].astype(F32) * SCALE
    on = jnp.dot(mask.astype(BF16), widen[...], preferred_element_type=F32)
    x = (pair[0:1] + FAR_AWAY * (1.0 - on)).astype(BF16)
    for a in range(mask.shape[0]):
        far_x[a] = x[a : a + 1]
    far_y[...] = pair[1:2].astype(BF16)


def block_of(slot, base, tile_row, j, near_x, near_y, far_x, far_y):
    rows = []
    for a in range(2):
        at = pl.ds(pl.multiple_of(base + a * TILE, TILE), TILE)
        x, y = near_x[slot, at, :], near_y[slot, at, :]
        row = []
        for b in range(2):
            across = pl.ds(j * BLOCK + b * TILE, TILE)
            row.append(kernel_of(x - far_x[tile_row + a, :, across], y - far_y[:, across]))
        rows.append(jnp.concatenate(row, axis=1))
    return jnp.concatenate(rows, axis=0)


def batches_of(n_row, n_col):
    cover, units = cover_of(n_row, n_col), list(units_of(n_row, n_col))
    start = len(cover) // 2
    order = [start] + [s for s in range(len(cover) - 1, 0, -1) if s != start]
    result, waited = [], {0}
    for slot in order:
        mine = sorted((u for u in units if slot in u), key=lambda u: (sum(u) - slot, u))
        units = [u for u in units if slot not in u]
        pieces = [mine]
        if slot == start:
            others = sorted({sum(u) - slot for u in mine})
            rest = len(others) - 1
            cuts = [0, 1] + [1 + k * rest // 3 for k in (1, 2, 3)]
            pieces = [
                [u for u in mine if sum(u) - slot in others[a:b]] for a, b in zip(cuts, cuts[1:])
            ]
            pieces = [piece for piece in pieces if piece]
        for k, piece in enumerate(pieces):
            need = sorted({s for u in piece for s in u} - waited)
            waited |= set(need)
            result.append((need, piece, slot if k == len(pieces) - 1 else None))
    return result


def tables_of(n_row, n_col):
    cover, batches = cover_of(n_row, n_col), batches_of(n_row, n_col)
    every = [u for _, units, _ in batches for u in units]
    result, seen, done = [], {(0, 0)}, 0
    for count in [1] + [len(units) for _, units, _ in batches]:
        reach = every[: done + 1] if not result else every[: done + count + 1]
        done += count if result else 0
        used = [o for i, j in reach for o in ((i, j), (j, i))]
        used = [(cover[i][0], cover[j][1]) for i, j in used]
        new = [o for o in dict.fromkeys(used) if o not in seen]
        seen |= set(new)
        result.append(new)
    return result


def step_kernel(
    n_row,
    n_col,
    direction,
    residual,
    positions,
    tile_pairs,
    count,
    applied,
    gram,
    dirs,
    places,
    tables,
    acc,
    near_x,
    near_y,
    far_x,
    far_y,
    widen,
    parts,
    land,
    gram_own,
    gram_half,
    gram_col,
    gram_row,
    *sems,
):
    ring = Ring(n_row, n_col)
    cover, holders = cover_of(n_row, n_col), holders_of(n_row, n_col)
    slots, probes, points = dirs.shape
    tiles, blocks = points // TILE, points // BLOCK
    half = blocks // 2
    group = group_of(n_row, n_col, tiles)
    scale = AMPLITUDE / 256.0
    me = ring.flat((ring.row, ring.col))

    ring.greet()
    dirs[0] = direction[...].astype(BF16)
    places[0] = positions[...]
    table, own_table = pattern(ring, tiles, group, tile_pairs, count[0])
    tables[me] = table.reshape(tables.shape[1:]).astype(BF16)
    ring.wait_greeted()
    batches, wanted = batches_of(n_row, n_col), tables_of(n_row, n_col)
    sends = []
    for s, offset in enumerate(cover[1:], 1):
        place = ring.minus(offset)
        sends.append(remote(places.at[0], places.at[s], sems[2].at[s], sems[3].at[s], place))

    def send_tables(offsets):
        for offset in offsets:
            k, at = holders.index(offset), tables.at[me]
            sends.append(remote(at, at, sems[0].at[k], sems[1].at[k], ring.minus(offset)))

    def wait_tables(offsets):
        for offset in offsets:
            k, origin = holders.index(offset), ring.plus(offset)
            at = tables.at[ring.flat(origin)]
            remote(at, at, sems[0].at[k], sems[1].at[k], origin).wait_recv()

    send_tables(wanted[0])
    for (need, _, _), offsets in zip(batches, wanted[1:]):
        for s in need:
            place = ring.minus(cover[s])
            sends.append(remote(dirs.at[0], dirs.at[s], sems[4].at[s], sems[5].at[s], place))
        send_tables(offsets)
    for copy in sends:
        copy.start()

    def exchanges(part):
        base = 8 + 4 * part
        over_col = Exchange(
            "col", n_col, gram_own.at[part], gram_col.at[part], sems[base], sems[base + 1]
        )
        over_row = Exchange(
            "row", n_row, gram_half.at[part], gram_row.at[part], sems[base + 2], sems[base + 3]
        )
        return over_col, over_row

    def sum_cols(part):
        total = gram_own[part]
        for k in range(1, n_col):
            total += gram_col[part, lax.rem(ring.col + k, n_col)]
        gram_half[part] = total

    def sum_rows(part):
        total = gram_half[part]
        for k in range(1, n_row):
            total += gram_row[part, lax.rem(ring.row + k, n_row)]
        gram[part * probes : (part + 1) * probes] = total

    def padded(product, before):
        widths = (before, TILE - before - product.shape[1])
        sides = [[jnp.zeros((probes, n), F32)] if n else [] for n in widths]
        return jnp.concatenate(sides[0] + [product] + sides[1], axis=1)

    early_col, early_row = exchanges(1)
    late_col, late_row = exchanges(0)
    sides = jnp.concatenate([residual[...], direction[...]], axis=0)
    gram_own[1] = padded(cross_gram_matrix(residual[...], sides), probes)
    early_col.start()

    acc[...] = jnp.zeros_like(acc)
    lane = lax.broadcasted_iota(jnp.int32, widen.shape, 1) >> log2(TILE)
    widen[...] = jnp.where(lane == lax.broadcasted_iota(jnp.int32, widen.shape, 0), 1.0, 0.0).astype(
        BF16
    )
    spread_places(0, places, near_x, near_y)
    set_far(0, own_table, places, widen, far_x, far_y)

    @pl.loop(0, blocks)
    def _(i):
        base = pl.multiple_of(i * BLOCK, BLOCK)
        total = jnp.zeros((probes, BLOCK), F32)
        for j in range(blocks):
            block = block_of(0, base, 2 * i, j, near_x, near_y, far_x, far_y)
            total += times_transposed(dirs[0, :, j * BLOCK : (j + 1) * BLOCK], block)
        acc[0, :, pl.ds(base, BLOCK)] += total

    for s, offset in enumerate(cover[1:], 1):
        origin = ring.plus(offset)
        remote(places.at[0], places.at[s], sems[2].at[s], sems[3].at[s], origin).wait_recv()

    @pl.loop(1, slots)
    def _(slot):
        spread_places(slot, places, near_x, near_y)

    wait_tables(wanted[0])
    rows_of, cols_of = [o[0] for o in cover], [o[1] for o in cover]

    def prepare(i, j):
        row_i, col_i = ring.plus((pick(i, rows_of), pick(i, cols_of)))
        row_j, col_j = ring.plus((pick(j, rows_of), pick(j, cols_of)))
        swap = (row_i * n_col + col_i - row_j * n_col - col_j + n_row * n_col) // (n_row * n_col)
        low, high = i + swap * (j - i), j + swap * (i - j)
        row_low = row_i + swap * (row_j - row_i)
        row_high = row_j + swap * (row_i - row_j)
        col_low = col_i + swap * (col_j - col_i)
        col_high = col_j + swap * (col_i - col_j)
        table = tables[row_low * n_col + col_high, col_low // group].astype(F32)
        lanes = table.shape[1]
        start = (col_low % group) * (n_row * tiles) + row_high * tiles
        mask = pltpu.roll(table, lax.rem(lanes - start, lanes), 1)
        set_far(high, mask[:, :TILE], places, widen, far_x, far_y)
        return low, high, swap * half

    def unit(low, high, first):
        forward = [None] * half
        backward = [None] * blocks
        for a in range(half):
            base = pl.multiple_of((first + a) * BLOCK, BLOCK)
            near_vec = dirs[low, :, pl.ds(base, BLOCK)]
            for b in range(blocks):
                block = block_of(low, base, 2 * (first + a), b, near_x, near_y, far_x, far_y)
                ahead = times_transposed(dirs[high, :, b * BLOCK : (b + 1) * BLOCK], block)
                back = jnp.dot(near_vec, block, preferred_element_type=F32)
                forward[a] = ahead if b == 0 else forward[a] + ahead
                backward[b] = back if a == 0 else backward[b] + back
        for a in range(half):
            base = pl.multiple_of((first + a) * BLOCK, BLOCK)
            acc[low, :, pl.ds(base, BLOCK)] += forward[a]
        for b in range(blocks):
            acc[high, :, b * BLOCK : (b + 1) * BLOCK] += backward[b]

    every = [u for _, units, _ in batches for u in units]
    state = prepare(jnp.int32(every[0][0]), jnp.int32(every[0][1]))
    done = 0
    for k, (need, units, complete) in enumerate(batches):
        for s in need:
            origin = ring.plus(cover[s])
            remote(dirs.at[0], dirs.at[s], sems[4].at[s], sems[5].at[s], origin).wait_recv()
        wait_tables(wanted[k + 1])
        done += len(units)
        coming = units[1:] + [every[done % len(every)]]

        def one(t, now):
            unit(*now)
            return prepare(pick(t, [u[0] for u in coming]), pick(t, [u[1] for u in coming]))

        state = lax.fori_loop(0, len(units), one, state)

        if k == len(batches) // 3:
            early_col.wait_recv()
            sum_cols(1)
            early_row.start()
        if k == 2 * len(batches) // 3:
            early_row.wait_recv()
            sum_rows(1)
        if complete is not None:
            s = complete - 1
            parts[s] = (scale * acc[complete]).astype(BF16)
            copy = remote(
                parts.at[s], land.at[s], sems[6].at[s], sems[7].at[s], ring.plus(cover[complete])
            )
            copy.start()
            sends.append(copy)

    image = scale * acc[0] + NUGGET * direction[...]
    for s, offset in enumerate(cover[1:]):
        origin = ring.minus(offset)
        remote(parts.at[s], land.at[s], sems[6].at[s], sems[7].at[s], origin).wait_recv()
        image += land[s].astype(F32)
    applied[...] = image
    gram_own[0] = padded(cross_gram_matrix(image, jnp.concatenate([image, sides], axis=0)), 0)
    late_col.start()
    late_col.wait_recv()
    sum_cols(0)
    late_row.start()
    late_row.wait_recv()
    sum_rows(0)
    for copy in sends + [early_col, early_row, late_col, late_row]:
        copy.wait_send()


class Exchange:
    def __init__(self, axis, size, source, landing, send_sem, recv_sem):
        self.axis, self.size, self.source, self.landing = axis, size, source, landing
        self.send_sem, self.recv_sem = send_sem, recv_sem
        self.me = lax.axis_index(axis)

    def copy(self, k, source, slot, peer):
        return pltpu.make_async_remote_copy(
            src_ref=source,
            dst_ref=self.landing.at[slot],
            send_sem=self.send_sem.at[k],
            recv_sem=self.recv_sem.at[k],
            device_id={self.axis: peer},
            device_id_type=MESH,
        )

    def outgoing(self, k):
        peer = lax.rem(self.me + k, self.size)
        return self.copy(k, self.source, self.me, peer)

    def start(self):
        for k in range(1, self.size):
            self.outgoing(k).start()

    def wait_recv(self):
        for k in range(1, self.size):
            origin = lax.rem(self.me + self.size - k, self.size)
            self.copy(k, self.landing.at[origin], origin, origin).wait_recv()

    def wait_send(self):
        for k in range(1, self.size):
            self.outgoing(k).wait_send()


def on_device(solution_field, residual, direction, positions, tile_pairs, pair_count):
    probes, points = direction.shape
    n_row, n_col = lax.axis_size("row"), lax.axis_size("col")
    cover, holders = cover_of(n_row, n_col), holders_of(n_row, n_col)
    slots, tiles = len(cover), points // TILE
    group = group_of(n_row, n_col, tiles)
    lanes = group * n_row * tiles
    vmem = pl.BlockSpec(memory_space=pltpu.VMEM)
    smem = pl.BlockSpec(memory_space=pltpu.SMEM)
    dma = pltpu.SemaphoreType.DMA
    applied, gram = pl.pallas_call(
        functools.partial(step_kernel, n_row, n_col),
        out_shape=(
            jax.ShapeDtypeStruct((probes, points), F32),
            jax.ShapeDtypeStruct((2 * probes, TILE), F32),
        ),
        in_specs=[vmem] * 4 + [smem],
        out_specs=(vmem, vmem),
        scratch_shapes=[
            pltpu.VMEM((slots, probes, points), BF16),
            pltpu.VMEM((slots, 2, points), BF16),
            pltpu.VMEM((n_row * n_col, n_col // group, tiles, lanes), BF16),
            pltpu.VMEM((slots, probes, points), F32),
            pltpu.VMEM((slots, points, TILE), BF16),
            pltpu.VMEM((slots, points, TILE), BF16),
            pltpu.VMEM((tiles, 1, points), BF16),
            pltpu.VMEM((1, points), BF16),
            pltpu.VMEM((TILE, points), BF16),
            pltpu.VMEM((slots - 1, probes, points), BF16),
            pltpu.VMEM((slots - 1, probes, points), BF16),
            pltpu.VMEM((2, probes, TILE), F32),
            pltpu.VMEM((2, probes, TILE), F32),
            pltpu.VMEM((2, n_col, probes, TILE), F32),
            pltpu.VMEM((2, n_row, probes, TILE), F32),
        ]
        + [dma((len(holders),))] * 2
        + [dma((slots,))] * 4
        + [dma((slots - 1,))] * 2
        + [dma((n_col,)), dma((n_col,)), dma((n_row,)), dma((n_row,))] * 2,
        compiler_params=pltpu.CompilerParams(collective_id=0, has_side_effects=True),
        name="step",
    )(direction, residual, positions, tile_pairs, pair_count)
    return pl.pallas_call(
        update_kernel,
        out_shape=(jax.ShapeDtypeStruct((probes, points), F32),) * 3,
        in_specs=[vmem] * 5,
        out_specs=(vmem,) * 3,
        name="update",
    )(gram, applied, solution_field, residual, direction)


def solution(mesh):
    whole = P(None, ("row", "col"))
    return jax.shard_map(
        on_device,
        mesh=mesh,
        in_specs=(whole, whole, whole, whole, whole, P(("row", "col"))),
        out_specs=(whole, whole, whole),
        check_vma=False,
    )
```
